128 devices in a mesh: lat: 8 (over x, core), lon: 16 (over y, z).
Axes of the slice: x: 4, y: 4, z: 4, core: 2. Of those that a mesh axis runs over, the one named last changes fastest.
Arguments:
- nodes: bfloat16 [8, 16, 384, 512], P('lat', 'lon'), may hold values from -6 to 6
- edges: bfloat16 [8, 16, 3072, 512], P('lat', 'lon'), may hold values from -6 to 6
- senders: int32 [8, 16, 3072], P('lat', 'lon'), may hold values from 0 to 607, as said below
- receivers: int32 [8, 16, 3072], P('lat', 'lon'), may hold values from 0 to 383
- edge_count: int32 [8, 16], P('lat', 'lon'), may hold values from 1536 to 3072, as said below
- halo_send: int32 [8, 16, 4, 24], P('lat', 'lon'), may hold values from 0 to 383
- long_need: int32 [8, 16, 128, 1], P('lat', 'lon'), may hold values from 0 to 1
- node_cot: bfloat16 [8, 16, 384, 512], P('lat', 'lon'), may hold values from -6 to 6
- edge_cot: bfloat16 [8, 16, 3072, 512], P('lat', 'lon'), may hold values from -6 to 6
- e_w1: bfloat16 [1536, 512], replicated, may hold values from -0.15625 to 0.15625
- e_b1: float32 [512], replicated, may hold values from -3 to 3
- e_w2: bfloat16 [512, 512], replicated, may hold values from -0.25 to 0.25
- e_gain: float32 [512], replicated, may hold values from 0.25 to 1.75
- n_w1: bfloat16 [1024, 512], replicated, may hold values from -0.1875 to 0.1875
- n_b1: float32 [512], replicated, may hold values from -3 to 3
- n_w2: bfloat16 [512, 512], replicated, may hold values from -0.25 to 0.25
- n_gain: float32 [512], replicated, may hold values from 0.25 to 1.75
Outputs:
- new_nodes: bfloat16 [8, 16, 384, 512], P('lat', 'lon')
- new_edges: bfloat16 [8, 16, 3072, 512], P('lat', 'lon')
- node_grad: float32 [8, 16, 384, 512], P('lat', 'lon')
- edge_grad: float32 [8, 16, 3072, 512], P('lat', 'lon')
- e_w1_grad: float32 [1536, 512], P(('lat', 'lon'))
- e_b1_grad: float32 [512], P(('lat', 'lon'))
- e_w2_grad: float32 [512, 512], P(('lat', 'lon'))
- e_gain_grad: float32 [512], P(('lat', 'lon'))
- n_w1_grad: float32 [1024, 512], P(('lat', 'lon'))
- n_b1_grad: float32 [512], P(('lat', 'lon'))
- n_w2_grad: float32 [512, 512], P(('lat', 'lon'))
- n_gain_grad: float32 [512], P(('lat', 'lon'))
The draws below stay inside these ranges and needn't reach their ends.
Inputs may be any that keep to these rules, and one draw needn't show every extreme that they name: `senders`: entries below 384 are a region's own nodes, the next 96 the four neighbour blocks, the rest the coarse rows; the third block is never named in the first band and the fourth never in the last. The first three edge slots of region r name the coarse rows of regions r + 1, r - 1 and r + 64 in flat order, counted round. `edge_count`: some region has all 3072 slots live. `long_need`: A region's coarse nodes are its first 2 rows.
All inputs are finite; a program needn't handle non-finite values.
Results may differ from the reference program's by a relative error of at most 0.009.
Values may be sent and summed in bfloat16 or wider, within the bound.
No kernel may reach another device: no remote copies, remote signals or barrier semaphores. Data moves between devices by JAX's collectives and lax.ppermute only.
A program may use at most 192 MiB of HBM per device.

```python
import jax
import jax.numpy as jnp
from jax import lax

D = 512
H = 512
NODE_DEV = 384
HALO = 24
COARSE = 2
LONG_SLOT = 1
E_DEV = 3072
N_LAT = 8
N_LON = 16
DEVICES = 128


def draw_senders(key, part):
    keys = jax.random.split(jax.random.fold_in(key, 11), 5)
    shape = (N_LAT, N_LON, E_DEV)
    regions = N_LAT * N_LON
    kind = jax.random.randint(keys[0], shape, 0, 100)
    local = jax.random.randint(keys[1], shape, 0, NODE_DEV)
    block = jax.random.randint(keys[2], shape, 0, 4)
    band = jnp.arange(N_LAT).reshape(N_LAT, 1, 1)
    block = jnp.where((block == 2) & (band == 0), 0, block)
    block = jnp.where((block == 3) & (band == N_LAT - 1), 1, block)
    halo = NODE_DEV + block * HALO + jax.random.randint(keys[3], shape, 0, HALO)
    far = NODE_DEV + 4 * HALO + jax.random.randint(keys[4], shape, 0, regions * LONG_SLOT)
    picked = jnp.where(kind < 80, local, jnp.where(kind < 97, halo, far))
    flat_index = jnp.arange(regions, dtype=jnp.int32).reshape(N_LAT, N_LON, 1)
    offsets = jnp.array([1, regions - 1, regions // 2], dtype=jnp.int32).reshape(1, 1, 3)
    source = (flat_index + offsets) % regions
    fixed_rows = NODE_DEV + 4 * HALO + source * LONG_SLOT
    slot = jnp.arange(E_DEV, dtype=jnp.int32).reshape(1, 1, E_DEV)
    padded = jnp.concatenate([fixed_rows, jnp.zeros((N_LAT, N_LON, E_DEV - 3), jnp.int32)], axis=2)
    return jnp.where(slot < 3, padded, picked).astype(jnp.int32)


def draw_edge_count(key, part):
    keys = jax.random.split(jax.random.fold_in(key, 23), 2)
    counts = jax.random.randint(keys[0], (N_LAT * N_LON,), E_DEV // 2, E_DEV + 1)
    fullest = jax.random.randint(keys[1], (), 0, N_LAT * N_LON)
    counts = jnp.where(jnp.arange(N_LAT * N_LON) == fullest, E_DEV, counts)
    return counts.reshape(N_LAT, N_LON).astype(jnp.int32)


def touch_ends(values, rng, least, top_value):
    longest = values.shape.index(max(values.shape))
    spots = []
    for shift in (0, 1):
        where = [jax.random.randint(jax.random.fold_in(rng, axis), (), 0, length) for axis, length in enumerate(values.shape)]
        where[longest] = (where[longest] + shift) % values.shape[longest]
        spots.append(tuple(where))
    return values.at[spots[0]].set(least).at[spots[1]].set(top_value)


def block_levels(own_key, extent, cuts, least, largest):
    level, own = 1.0, jax.random.fold_in(own_key, 6)
    for dim, blocks in cuts:
        steps = jnp.exp(jax.random.uniform(jax.random.fold_in(own, dim), (blocks,), jnp.float32, least / len(cuts), largest / len(cuts)))
        level = level * jnp.repeat(steps, extent[dim] // blocks).reshape([-1 if axis == dim else 1 for axis in range(len(extent))])
    return level


def noise(key, dims, scale, most, cuts=(), kind=jnp.bfloat16):
    values = scale * jax.random.normal(key, dims, jnp.float32)
    if cuts:
        values = values * block_levels(key, dims, cuts, -0.22, 0.18)
    return jnp.clip(values, -most, most).astype(kind)


def setup_inputs(seed: int = 0) -> dict:
    key_of = jax.random.split(jax.random.key(seed), 18)
    nodes = noise(key_of[0], (N_LAT, N_LON, NODE_DEV, D), 1.0, 6.0, ((0, 8), (1, 16)))
    edges = noise(key_of[1], (N_LAT, N_LON, E_DEV, D), 1.0, 6.0, ((0, 8), (1, 16)))
    senders = draw_senders(jax.random.fold_in(key_of[17], 71), 0)
    receivers = touch_ends(jax.random.randint(key_of[3], (N_LAT, N_LON, E_DEV), 0, NODE_DEV), jax.random.fold_in(key_of[3], 1), 0, NODE_DEV - 1).astype(jnp.int32)
    edge_count = draw_edge_count(jax.random.fold_in(key_of[17], 71), 0)
    halo_send = touch_ends(jax.random.randint(key_of[5], (N_LAT, N_LON, 4, HALO), 0, NODE_DEV), jax.random.fold_in(key_of[5], 1), 0, NODE_DEV - 1).astype(jnp.int32)
    long_need = touch_ends(jax.random.randint(key_of[6], (N_LAT, N_LON, DEVICES, LONG_SLOT), 0, COARSE), jax.random.fold_in(key_of[6], 1), 0, COARSE - 1).astype(jnp.int32)
    node_cot = noise(key_of[7], (N_LAT, N_LON, NODE_DEV, D), 1.0, 6.0, ((0, 8), (1, 16)))
    edge_cot = noise(key_of[8], (N_LAT, N_LON, E_DEV, D), 1.0, 6.0, ((0, 8), (1, 16)))
    e_w1 = noise(key_of[9], (3 * D, H), (3 * D) ** -0.5, 0.15625)
    e_b1 = noise(key_of[10], (H,), 0.5, 3.0, (), jnp.float32)
    e_w2 = noise(key_of[11], (H, D), H ** -0.5, 0.25)
    e_gain = jnp.clip(1.0 + 0.15 * jax.random.normal(key_of[12], (D,), jnp.float32), 0.25, 1.75)
    n_w1 = noise(key_of[13], (2 * D, H), (2 * D) ** -0.5, 0.1875)
    n_b1 = noise(key_of[14], (H,), 0.5, 3.0, (), jnp.float32)
    n_w2 = noise(key_of[15], (H, D), H ** -0.5, 0.25)
    n_gain = jnp.clip(1.0 + 0.15 * jax.random.normal(key_of[16], (D,), jnp.float32), 0.25, 1.75)
    return {"nodes": nodes, "edges": edges, "senders": senders, "receivers": receivers, "edge_count": edge_count, "halo_send": halo_send, "long_need": long_need, "node_cot": node_cot, "edge_cot": edge_cot, "e_w1": e_w1, "e_b1": e_b1, "e_w2": e_w2, "e_gain": e_gain, "n_w1": n_w1, "n_b1": n_b1, "n_w2": n_w2, "n_gain": n_gain}


EPS = 1e-05

def layer_norm(z, gain):
    mean = lax.optimization_barrier(jnp.mean(z, axis=-1, keepdims=True))
    centred = z - mean
    rstd = lax.rsqrt(lax.optimization_barrier(jnp.mean(centred * centred, axis=-1, keepdims=True)) + EPS)
    normed = centred * rstd
    return (normed * gain, normed, rstd)

def transposed(left, right):
    return lax.dot_general(left, right, (((0,), (0,)), ((), ())), preferred_element_type=jnp.float32)

def mlp_forward(parts, w_first, b_first, w_second, gain):
    joined = jnp.concatenate(parts, axis=1)
    z_first = jnp.dot(joined, w_first, preferred_element_type=jnp.float32) + b_first
    active = jax.nn.silu(z_first).astype(jnp.bfloat16)
    z_second = jnp.dot(active, w_second, preferred_element_type=jnp.float32)
    result, normed, rstd = layer_norm(z_second, gain)
    return (result, (z_first, active, normed, rstd))

def mlp_backward(parts, saved, grad_out, w_first, w_second, gain):
    z_first, active, normed, rstd = saved
    gain_grad = lax.optimization_barrier(jnp.sum(grad_out * normed, axis=0))
    scaled = grad_out * gain
    g_second = rstd * (scaled - lax.optimization_barrier(jnp.mean(scaled, axis=-1, keepdims=True)) - normed * lax.optimization_barrier(jnp.mean(scaled * normed, axis=-1, keepdims=True)))
    g_second = g_second.astype(jnp.bfloat16)
    second_grad = transposed(active, g_second)
    g_active = jnp.dot(g_second, w_second.T, preferred_element_type=jnp.float32)
    sigma = jax.nn.sigmoid(z_first)
    g_first = (g_active * sigma * (1.0 + z_first * (1.0 - sigma))).astype(jnp.bfloat16)
    bias_grad = lax.optimization_barrier(jnp.sum(g_first, axis=0, dtype=jnp.float32))
    joined = jnp.concatenate(parts, axis=1)
    first_grad = transposed(joined, g_first)
    g_input = jnp.dot(g_first, w_first.T, preferred_element_type=jnp.float32)
    return (g_input, (first_grad, bias_grad, second_grad, gain_grad))

def device_pass(table, nodes_l, edges_l, snd, rcv, count, node_cot_l, edge_cot_l, weights):
    e_w1, e_b1, e_w2, e_gain, n_w1, n_b1, n_w2, n_gain = weights
    width = nodes_l.shape[1]
    node_n = nodes_l.shape[0]
    sent_rows = jnp.take(table, snd, axis=0)
    recv_rows = jnp.take(nodes_l, rcv, axis=0)
    edge_parts = (edges_l, sent_rows, recv_rows)
    edge_out, edge_saved = mlp_forward(edge_parts, e_w1, e_b1, e_w2, e_gain)
    alive = jnp.arange(edges_l.shape[0]) < count
    live = alive.astype(jnp.float32)[:, None]
    new_edges = (edges_l + live * edge_out).astype(jnp.bfloat16)
    recv_table = ((rcv[None, :] == jnp.arange(node_n)[:, None]) & alive[None, :]).astype(jnp.bfloat16)
    aggregate = jnp.dot(recv_table, new_edges, preferred_element_type=jnp.float32).astype(jnp.bfloat16)
    node_parts = (nodes_l, aggregate)
    node_out, node_saved = mlp_forward(node_parts, n_w1, n_b1, n_w2, n_gain)
    new_nodes = (nodes_l + node_out).astype(jnp.bfloat16)
    node_up = node_cot_l.astype(jnp.float32)
    g_node_in, node_grads = mlp_backward(node_parts, node_saved, node_up, n_w1, n_w2, n_gain)
    g_aggregate = g_node_in[:, width:]
    g_new_edges = edge_cot_l.astype(jnp.float32) + live * jnp.take(g_aggregate, rcv, axis=0)
    g_edge_in, edge_grads = mlp_backward(edge_parts, edge_saved, live * g_new_edges, e_w1, e_w2, e_gain)
    g_edge_in = g_edge_in.astype(jnp.bfloat16)
    edge_grad = g_new_edges + g_edge_in[:, :width]
    node_local = node_up + g_node_in[:, :width] + jnp.dot(recv_table, g_edge_in[:, 2 * width:], preferred_element_type=jnp.float32)
    send_table = (snd[None, :] == jnp.arange(table.shape[0])[:, None]).astype(jnp.bfloat16)
    sender_grad = jnp.dot(send_table, g_edge_in[:, width:2 * width], preferred_element_type=jnp.float32)
    return (new_nodes, new_edges, edge_grad, node_local, sender_grad, edge_grads + node_grads)

def pick_rows(source, rows):
    return jnp.take(source, rows, axis=0)

def add_rows(rows, values, node_n, width):
    return jnp.zeros((node_n, width), jnp.float32).at[rows].add(values)

def reference(nodes, edges, senders, receivers, edge_count, halo_send, long_need, node_cot, edge_cot, e_w1, e_b1, e_w2, e_gain, n_w1, n_b1, n_w2, n_gain):
    lat_n, lon_n, node_n, width = nodes.shape
    devices = lat_n * lon_n
    halo_n = halo_send.shape[3]
    slot_n = long_need.shape[3]
    sent = jax.vmap(jax.vmap(pick_rows))(nodes, halo_send)
    zero_band = jnp.zeros_like(sent[:1, :, 2])
    block_east = jnp.roll(sent[:, :, 0], 1, axis=1)
    block_west = jnp.roll(sent[:, :, 1], -1, axis=1)
    block_north = jnp.concatenate([zero_band, sent[:-1, :, 2]], axis=0)
    block_south = jnp.concatenate([sent[1:, :, 3], zero_band], axis=0)
    halo = jnp.stack([block_east, block_west, block_north, block_south], axis=2).reshape(lat_n, lon_n, 4 * halo_n, width)
    coarse = nodes[:, :, :COARSE].reshape(devices * COARSE, width)
    far_ids = (jnp.arange(devices, dtype=jnp.int32)[:, None] * COARSE + long_need).reshape(lat_n, lon_n, devices * slot_n)
    far = jnp.take(coarse, far_ids, axis=0)
    table = jnp.concatenate([nodes, halo, far], axis=2).reshape(devices, -1, width)
    weights = (e_w1, e_b1, e_w2, e_gain, n_w1, n_b1, n_w2, n_gain)

    def flat(array):
        return array.reshape((devices,) + array.shape[2:])
    inputs = (table, flat(nodes), flat(edges), flat(senders), flat(receivers), edge_count.reshape(devices), flat(node_cot), flat(edge_cot))
    init = tuple((jnp.zeros(weight.shape, jnp.float32) for weight in weights))

    def step(carry, item):
        new_nodes, new_edges, edge_grad, node_local, sender_grad, grads = device_pass(*item, weights)
        carry = tuple((total + grad for total, grad in zip(carry, grads)))
        return (carry, (new_nodes, new_edges, edge_grad, node_local, sender_grad))
    sums, outputs = lax.scan(step, init, inputs)
    new_nodes, new_edges, edge_grad, node_local, sender_grad = outputs
    sender_grad = sender_grad.reshape(lat_n, lon_n, -1, width)
    halo_grad = sender_grad[:, :, node_n:node_n + 4 * halo_n].reshape(lat_n, lon_n, 4, halo_n, width)
    far_grad = sender_grad[:, :, node_n + 4 * halo_n:]
    zero_grad = jnp.zeros_like(halo_grad[:1, :, 2])
    back_east = jnp.roll(halo_grad[:, :, 0], -1, axis=1)
    back_west = jnp.roll(halo_grad[:, :, 1], 1, axis=1)
    back_north = jnp.concatenate([halo_grad[1:, :, 2], zero_grad], axis=0)
    back_south = jnp.concatenate([zero_grad, halo_grad[:-1, :, 3]], axis=0)
    back = jnp.stack([back_east, back_west, back_north, back_south], axis=2).reshape(lat_n, lon_n, 4 * halo_n, width)
    node_grad = node_local.reshape(lat_n, lon_n, node_n, width) + sender_grad[:, :, :node_n]
    returned = jax.vmap(jax.vmap(lambda rows, values: add_rows(rows, values, node_n, width)))(halo_send.reshape(lat_n, lon_n, 4 * halo_n), back)
    node_grad = node_grad + returned
    coarse_grad = jax.ops.segment_sum(far_grad.reshape(-1, width), far_ids.reshape(-1), num_segments=devices * COARSE)
    node_grad = node_grad.at[:, :, :COARSE].add(coarse_grad.reshape(lat_n, lon_n, COARSE, width))
    return (new_nodes.reshape(nodes.shape), new_edges.reshape(edges.shape), node_grad, edge_grad.reshape(edges.shape), sums[0], sums[1], sums[2], sums[3], sums[4], sums[5], sums[6], sums[7])
```

```python
import functools

import jax
import jax.numpy as jnp
from jax import lax
from jax.experimental import pallas as pl
from jax.experimental.pallas import tpu as pltpu
from jax.sharding import Mesh
from jax.sharding import PartitionSpec as P

COARSE = 2
LON = ("lon_0", "lon_1")
LAT = ("lat_0", "lat_1")
LAT_LON = ("lat_0", "lat_1", "lon_0", "lon_1")
EPS = 1e-05
BF = jnp.bfloat16
F32 = jnp.float32

NODES = 384
HALO = 24
WIDE = 512
EDGES = 3072
FAR = 128
BLOCK = 768
STEPS = EDGES // BLOCK
SENDERS = 640
ONES_ROW = 608
TABLE = SENDERS + NODES
FIRST = WIDE + SENDERS
GROUPS = 32
GROUP_ROWS = 128


def mm(a, b):
    return lax.dot_general(a, b, (((1,), (0,)), ((), ())), preferred_element_type=F32)


def mm_t(a, b):
    return lax.dot_general(a, b, (((1,), (1,)), ((), ())), preferred_element_type=F32)


def t_mm(a, b):
    return lax.dot_general(a, b, (((0,), (0,)), ((), ())), preferred_element_type=F32)


def row_mean(v):
    return jnp.sum(v, axis=1, keepdims=True) * (1.0 / WIDE)


def first_act(z):
    sig = 0.5 + 0.5 * jnp.tanh(0.5 * z)
    act = z * sig
    return act, sig + act * (1.0 - sig)


def normalise(z):
    centred = z - row_mean(z)
    rstd = lax.rsqrt(row_mean(centred * centred) + EPS)
    return centred * rstd, rstd


def norm_back(g, normed, rstd, gain):
    s = g * gain
    return rstd * (s - row_mean(s) - normed * row_mean(s * normed))


def lane_ids(row):
    return jnp.transpose(jnp.broadcast_to(row, (128, BLOCK)))


def hot_lanes(ids, first, chunks):
    lane = lax.broadcasted_iota(jnp.int32, (BLOCK, 128), 1).astype(F32)
    return [
        jnp.where(ids == lane + float(first + 128 * j), 1.0, 0.0).astype(BF) for j in range(chunks)
    ]


def spread_kernel(nodes_ref, coarse_ref):
    coarse_ref[...] = jnp.broadcast_to(nodes_ref[0:COARSE][None], (FAR, COARSE, WIDE))


def spread(nodes):
    return pl.pallas_call(
        spread_kernel,
        name="spread_coarse",
        grid=(1,),
        in_specs=[pl.BlockSpec((16, WIDE), lambda i: (0, 0))],
        out_specs=pl.BlockSpec((FAR, COARSE, WIDE), lambda i: (0, 0, 0)),
        out_shape=jax.ShapeDtypeStruct((FAR, COARSE, WIDE), BF),
    )(nodes)


def border_kernel(nodes_ref, rows_ref, *sent_refs):
    at = lax.broadcasted_iota(jnp.int32, (NODES, HALO), 0)
    for k, sent_ref in enumerate(sent_refs):
        hot = jnp.where(at == rows_ref[k : k + 1], 1.0, 0.0).astype(BF)
        sent_ref[...] = t_mm(hot, nodes_ref[...]).astype(BF)


def borders(nodes, rows_out):
    return pl.pallas_call(
        border_kernel,
        name="border_rows",
        out_shape=[jax.ShapeDtypeStruct((HALO, WIDE), BF)] * 4,
        cost_estimate=pl.CostEstimate(
            flops=8 << 30, transcendentals=0, bytes_accessed=8 << 20
        ),
    )(nodes, rows_out)


def whole(*shape):
    return pl.BlockSpec(shape, lambda i: (0,) * len(shape), pipeline_mode=pl.Buffered(1))


def by_block(shape, pick):
    return pl.BlockSpec(shape, lambda i: (pick(i),) + (0,) * (len(shape) - 1))


def params():
    return pltpu.CompilerParams(
        dimension_semantics=("arbitrary",), vmem_limit_bytes=60 * 1024 * 1024
    )


def layer_kernel(
    place_ref,
    snd_ref,
    rcv_ref,
    need_ref,
    edges_ref,
    ecot_ref,
    nodes_ref,
    from_east_ref,
    from_west_ref,
    from_north_ref,
    from_south_ref,
    far_ref,
    ncot_ref,
    ew1_ref,
    ew2_ref,
    nw1_ref,
    nw2_ref,
    eb1_ref,
    eg_ref,
    nb1_ref,
    ng_ref,
    new_nodes_ref,
    new_edges_ref,
    gz_ref,
    gagg_ref,
    node_ref,
    east_ref,
    west_ref,
    north_ref,
    south_ref,
    keep_ref,
    send_ref,
    table_s,
    right_s,
    left_s,
    act_s,
    dact_s,
    normed_s,
    rstd_s,
    agg_s,
    gnode_s,
    dw1_s,
    dw2_s,
    gain_s,
    nvec_s,
    packed_s,
    sems,
):
    step = pl.program_id(0)
    count = place_ref[0]
    egain = eg_ref[...].reshape(1, WIDE)

    def out_copies(g):
        copies = []
        for other, ref in ((0, keep_ref), (1, send_ref)):
            group = (g >> 2) * 8 + (place_ref[1] ^ other) * 4 + (g & 3)
            copies.append(
                pltpu.make_async_copy(packed_s.at[group], ref.at[g], sems.at[2 * g + other])
            )
        return copies

    @pl.when(step == 0)
    def _():
        table_s[0:NODES] = nodes_ref[...]
        borders = (from_east_ref, from_west_ref, from_north_ref, from_south_ref)
        table_s[NODES : NODES + 96] = jnp.concatenate(
            [ref[...].astype(F32) for ref in borders], axis=0
        ).astype(BF)
        need = need_ref[...].astype(F32)
        pick = jnp.transpose(jnp.broadcast_to(need, (128, 128)))[:, 0:1]
        low, high = far_ref[:, 0].astype(F32), far_ref[:, 1].astype(F32)
        table_s[480:608] = jnp.where(pick == 0.0, low, high).astype(BF)
        table_s[608:SENDERS] = jnp.zeros((32, WIDE), BF)
        right_s[0:WIDE] = ew1_ref[0:WIDE]
        right_s[WIDE:FIRST] = mm(table_s[...], ew1_ref[WIDE : 2 * WIDE]).astype(BF)
        right_s[FIRST:] = mm(nodes_ref[...], ew1_ref[2 * WIDE :]).astype(BF)
        agg_s[...] = jnp.zeros_like(agg_s)
        dw1_s[...] = jnp.zeros_like(dw1_s)
        dw2_s[...] = jnp.zeros_like(dw2_s)
        gain_s[...] = jnp.zeros_like(gain_s)

    @pl.when(step < STEPS)
    def _():
        at = pl.multiple_of(step * BLOCK, BLOCK)
        here = pl.ds(at, BLOCK)
        slot = lax.broadcasted_iota(jnp.int32, (1, BLOCK), 1) + at
        snd = snd_ref[0].astype(F32)
        rcv = jnp.where(slot < count, rcv_ref[0].astype(F32), -1.0)
        edges = edges_ref[...]
        left_s[here, 0:WIDE] = edges
        hots = hot_lanes(lane_ids(snd), 0, SENDERS // 128)
        lane = lax.broadcasted_iota(jnp.int32, (BLOCK, 128), 1)
        hots[4] = jnp.where(lane == ONES_ROW - 512, 1.0, hots[4].astype(F32)).astype(BF)
        hots += hot_lanes(lane_ids(rcv), 0, NODES // 128)
        for k, hot in enumerate(hots):
            left_s[here, WIDE + 128 * k : WIDE + 128 * (k + 1)] = hot
        z1 = mm(left_s[here], right_s[...]) + eb1_ref[...].reshape(1, WIDE)
        act, dact = first_act(z1)
        act = act.astype(BF)
        act_s[here] = act
        dact_s[here] = dact.astype(BF)
        normed, rstd = normalise(mm(act, ew2_ref[...]))
        normed_s[here] = normed.astype(BF)
        rstd_s[here] = jnp.broadcast_to(rstd, (BLOCK, 128))
        live = (lax.broadcasted_iota(jnp.int32, (BLOCK, 1), 0) + at < count).astype(F32)
        fresh = (edges.astype(F32) + (live * normed) * egain).astype(BF)
        new_edges_ref[...] = fresh
        agg_s[...] += t_mm(left_s[here, FIRST:], fresh)

    @pl.when(step == STEPS - 1)
    def _():
        nodes = nodes_ref[...]
        ngain = ng_ref[...].reshape(1, WIDE)
        agg = agg_s[...].astype(BF)
        z1 = mm(nodes, nw1_ref[0:WIDE]) + mm(agg, nw1_ref[WIDE:]) + nb1_ref[...].reshape(1, WIDE)
        act, dact = first_act(z1)
        act = act.astype(BF)
        normed, rstd = normalise(mm(act, nw2_ref[...]))
        new_nodes_ref[...] = (nodes.astype(F32) + normed * ngain).astype(BF)
        cot = ncot_ref[...].astype(F32)
        gz2 = norm_back(cot, normed, rstd, ngain).astype(BF)
        nvec_s[1:2] = jnp.sum(cot * normed, axis=0, keepdims=True)
        gz1 = (mm_t(gz2, nw2_ref[...]) * dact).astype(BF)
        nvec_s[0:1] = jnp.sum(gz1.astype(F32), axis=0, keepdims=True)
        packed_s[0:16, 0:32] = t_mm(nodes, gz1).astype(BF).reshape(16, 32, WIDE)
        packed_s[16:32, 0:32] = t_mm(agg, gz1).astype(BF).reshape(16, 32, WIDE)
        packed_s[:, 32:48] = t_mm(act, gz2).astype(BF).reshape(GROUPS, 16, WIDE)
        gnode_s[...] = cot + mm_t(gz1, nw1_ref[0:WIDE])
        gagg_ref[...] = mm_t(gz1, nw1_ref[WIDE:]).astype(BF)

    @pl.when(step >= STEPS)
    def _():
        at = pl.multiple_of((step - STEPS) * BLOCK, BLOCK)
        here = pl.ds(at, BLOCK)
        live = (lax.broadcasted_iota(jnp.int32, (BLOCK, 1), 0) + at < count).astype(F32)
        g = live * ecot_ref[...].astype(F32) + mm(left_s[here, FIRST:], gagg_ref[...])
        normed = normed_s[here].astype(F32)
        gain_s[...] += jnp.sum((g * normed).reshape(BLOCK // 8, 8, WIDE), axis=0)
        gz2 = norm_back(g, normed, rstd_s[here][:, 0:1], egain).astype(BF)
        dw2_s[...] += t_mm(act_s[here], gz2)
        gz1 = (mm_t(gz2, ew2_ref[...]) * dact_s[here].astype(F32)).astype(BF)
        gz_ref[...] = gz1
        dw1_s[...] += t_mm(left_s[here], gz1)

    @pl.when(step == 2 * STEPS - 1)
    def _():
        packed_s[:, 96:112] = dw2_s[...].astype(BF).reshape(GROUPS, 16, WIDE)
        sent, got = dw1_s[WIDE:FIRST].astype(BF), dw1_s[FIRST:].astype(BF)
        first = jnp.concatenate(
            [
                dw1_s[0:WIDE].astype(BF),
                t_mm(table_s[...], sent).astype(BF),
                t_mm(nodes_ref[...], got).astype(BF),
            ],
            axis=0,
        )
        packed_s[:, 48:96] = first.reshape(GROUPS, 48, WIDE)
        back = mm_t(sent, ew1_ref[WIDE : 2 * WIDE])
        vectors = (
            dw1_s[WIDE + ONES_ROW : WIDE + ONES_ROW + 1],
            jnp.sum(gain_s[...], axis=0, keepdims=True),
            nvec_s[0:1],
            nvec_s[1:2],
        )
        half = WIDE // 2
        paired = [
            jnp.concatenate([vectors[k][:, side], vectors[k + 1][:, side]], axis=1)
            for side in (slice(0, half), slice(half, WIDE))
            for k in (0, 2)
        ]
        extra = jnp.concatenate([back[480:608]] + paired + [jnp.zeros((124, WIDE), F32)], axis=0)
        out = lax.broadcasted_iota(jnp.int32, (GROUPS * 16, 256), 0)
        src = lax.broadcasted_iota(jnp.int32, (GROUPS * 16, 256), 1)
        need = jnp.concatenate([need_ref[...], jnp.zeros((1, 128), jnp.int32)], axis=1)
        slot = out & 15
        low = (slot < 4) & (src == (out >> 4) * 4 + slot) & (need == 0)
        high = (slot >= 4) & (slot < 8) & (src == (out >> 4) * 4 + slot - 4) & (need == 1)
        small = (slot >= 8) & (slot < 10) & (src == 120 + slot + (out >> 8) * 2)
        move = jnp.where(low | high | small, 1.0, 0.0).astype(BF)
        packed_s[:, 112:128] = mm(move, extra.astype(BF)).astype(BF).reshape(GROUPS, 16, WIDE)
        out = lax.broadcasted_iota(jnp.int32, (128, 128), 0)
        src = lax.broadcasted_iota(jnp.int32, (128, 128), 1)
        z, slot = out >> 5, out & 31
        want = jnp.where(slot < 8, 8 * z + slot, 24 + 4 * z + slot)
        want = jnp.where(slot >= 12, 36 + 12 * z + slot, want)
        want = jnp.where(slot >= 24, 72 + 4 * z + slot, want)
        want = jnp.where(slot >= 28, 112 + z + 4 * (slot - 28), want)
        want = jnp.where(slot >= 30, 90 + slot, want)
        order = jnp.where(src == want, 1.0, 0.0).astype(BF)
        for g in range(16):
            for group in ((g >> 2) * 8 + (g & 3), (g >> 2) * 8 + 4 + (g & 3)):
                packed_s[group] = mm(order, packed_s[group]).astype(BF)
            for copy in out_copies(g):
                copy.start()
        node_ref[...] = gnode_s[...] + back[0:NODES] + mm_t(got, ew1_ref[2 * WIDE :])
        for k, ref in enumerate((east_ref, west_ref, north_ref, south_ref)):
            ref[...] = back[NODES + HALO * k : NODES + HALO * (k + 1)].astype(BF)
        for g in range(16):
            for copy in out_copies(g):
                copy.wait()


def layer(place, snd, rcv, need, edges, ecot, nodes, borders, far, ncot, ew1, ew2, nw1, nw2, eb1, eg, nb1, ng):
    first = lambda i: jnp.minimum(i, STEPS - 1)
    later = lambda i: jnp.maximum(i - STEPS, 0)
    sds = jax.ShapeDtypeStruct
    return pl.pallas_call(
        layer_kernel,
        name="mesh_layer",
        grid=(2 * STEPS,),
        in_specs=[
            pl.BlockSpec(memory_space=pltpu.SMEM),
            by_block((1, 1, BLOCK), first),
            by_block((1, 1, BLOCK), first),
            whole(1, FAR),
            by_block((BLOCK, WIDE), first),
            by_block((BLOCK, WIDE), later),
            whole(NODES, WIDE),
            whole(HALO, WIDE),
            whole(HALO, WIDE),
            whole(HALO, WIDE),
            whole(HALO, WIDE),
            whole(FAR, COARSE, WIDE),
            whole(NODES, WIDE),
            whole(3 * WIDE, WIDE),
            whole(WIDE, WIDE),
            whole(2 * WIDE, WIDE),
            whole(WIDE, WIDE),
            whole(WIDE),
            whole(WIDE),
            whole(WIDE),
            whole(WIDE),
        ],
        out_specs=[
            whole(NODES, WIDE),
            by_block((BLOCK, WIDE), first),
            by_block((BLOCK, WIDE), later),
            whole(NODES, WIDE),
            whole(NODES, WIDE),
        ]
        + [whole(HALO, WIDE)] * 4
        + [pl.BlockSpec(memory_space=pl.ANY)] * 2,
        out_shape=[
            sds((NODES, WIDE), BF),
            sds((EDGES, WIDE), BF),
            sds((EDGES, WIDE), BF),
            sds((NODES, WIDE), BF),
            sds((NODES, WIDE), F32),
        ]
        + [sds((HALO, WIDE), BF)] * 4
        + [sds((16, GROUP_ROWS, WIDE), BF)] * 2,
        scratch_shapes=[
            pltpu.VMEM((SENDERS, WIDE), BF),
            pltpu.VMEM((WIDE + TABLE, WIDE), BF),
            pltpu.VMEM((EDGES, WIDE + TABLE), BF),
            pltpu.VMEM((EDGES, WIDE), BF),
            pltpu.VMEM((EDGES, WIDE), BF),
            pltpu.VMEM((EDGES, WIDE), BF),
            pltpu.VMEM((EDGES, 128), F32),
            pltpu.VMEM((NODES, WIDE), F32),
            pltpu.VMEM((NODES, WIDE), F32),
            pltpu.VMEM((WIDE + TABLE, WIDE), F32),
            pltpu.VMEM((WIDE, WIDE), F32),
            pltpu.VMEM((8, WIDE), F32),
            pltpu.VMEM((8, WIDE), F32),
            pltpu.VMEM((GROUPS, GROUP_ROWS, WIDE), BF),
            pltpu.SemaphoreType.DMA((32,)),
        ],
        compiler_params=params(),
        cost_estimate=pl.CostEstimate(
            flops=18 << 30, transcendentals=4 << 20, bytes_accessed=30 << 20
        ),
    )(place, snd, rcv, need, edges, ecot, nodes, *borders, far, ncot, ew1, ew2, nw1, nw2, eb1, eg, nb1, ng)


def edge_grad_kernel(count_ref, rcv_ref, ecot_ref, gz_ref, gagg_ref, ew1_ref, out_ref):
    at = pl.program_id(0) * BLOCK
    back = jnp.concatenate(hot_lanes(lane_ids(rcv_ref[0].astype(F32)), 0, NODES // 128), axis=1)
    live = (lax.broadcasted_iota(jnp.int32, (BLOCK, 1), 0) + at < count_ref[0]).astype(F32)
    taken = live * mm(back, gagg_ref[...])
    out_ref[...] = ecot_ref[...].astype(F32) + taken + mm_t(gz_ref[...], ew1_ref[...])


def edge_grads(place, rcv, ecot, gz, gagg, ew1):
    same = lambda i: i
    return pl.pallas_call(
        edge_grad_kernel,
        name="edge_grads",
        grid=(STEPS,),
        in_specs=[
            pl.BlockSpec(memory_space=pltpu.SMEM),
            by_block((1, 1, BLOCK), same),
            by_block((BLOCK, WIDE), same),
            by_block((BLOCK, WIDE), same),
            whole(NODES, WIDE),
            whole(WIDE, WIDE),
        ],
        out_specs=by_block((BLOCK, WIDE), same),
        out_shape=jax.ShapeDtypeStruct((EDGES, WIDE), F32),
        compiler_params=params(),
        cost_estimate=pl.CostEstimate(
            flops=2 * EDGES * WIDE * (WIDE + NODES), transcendentals=0, bytes_accessed=13 << 20
        ),
    )(place, rcv, ecot, gz, gagg, ew1)


def finish_kernel(lane_ref, total_ref, node_ref, out_ref, *grads):
    total = total_ref[...]
    ew1, eb1, ew2, eg, nw1, nb1, nw2, ng = grads
    nw1[...] = total[0:8]
    nw2[...] = total[8:12]
    ew1[...] = total[12:24]
    ew2[...] = total[24:28]
    out_ref[...] = node_ref[...]
    out_ref[0:COARSE] += total[28:30]
    half = WIDE // 2
    lines = [total[30:31, :half], total[30:31, half:], total[31:32, :half], total[31:32, half:]]
    lines = jnp.concatenate(lines + [jnp.zeros((4, half), F32)], axis=0)
    lines = pltpu.roll(lines, (half - lane_ref[0]) & (half - 1), 1)
    for k, ref in enumerate((eb1, eg, nb1, ng)):
        ref[...] = lines[k, 0:4]


def finish(lane, total, node_grad):
    sds = jax.ShapeDtypeStruct
    rows = [(12, WIDE), (4,), (4, WIDE), (4,), (8, WIDE), (4,), (4, WIDE), (4,)]
    first = pl.BlockSpec((8, WIDE), lambda i: (0, 0))
    return pl.pallas_call(
        finish_kernel,
        name="finish_grads",
        grid=(1,),
        in_specs=[
            pl.BlockSpec(memory_space=pltpu.SMEM),
            whole(GROUP_ROWS // 4, WIDE),
            first,
        ],
        out_specs=[first] + [pl.BlockSpec(r, lambda i, n=len(r): (0,) * n) for r in rows],
        out_shape=[sds((NODES, WIDE), F32)] + [sds(r, F32) for r in rows],
        input_output_aliases={2: 0},
        compiler_params=params(),
    )(lane, total, node_grad)


def ring(block, axis, distance):
    n = lax.axis_size(axis)
    return lax.ppermute(block, axis, [(i, (i + distance) % n) for i in range(n)])


def passed_along(value, axis, steps):
    count = lax.axis_size(axis)
    leading, last = (max(0, -steps), min(count, count - steps))
    return lax.ppermute(value, axis, [(source, source + steps) for source in range(leading, last)])


def shards(
    nodes,
    edges,
    senders,
    receivers,
    edge_count,
    halo_send,
    long_need,
    node_cot,
    edge_cot,
    e_w1,
    e_b1,
    e_w2,
    e_gain,
    n_w1,
    n_b1,
    n_w2,
    n_gain,
):
    nodes_l, edges_l, ecot = nodes[0, 0], edges[0, 0], edge_cot[0, 0]
    rows_out = halo_send[0, 0]
    snd = senders.reshape(STEPS, 1, BLOCK)
    rcv = receivers.reshape(STEPS, 1, BLOCK)
    far = lax.all_to_all(spread(nodes_l), LAT_LON, split_axis=0, concat_axis=0, tiled=True)
    sent = borders(nodes_l, rows_out)
    halo = [
        ring(sent[0], LON, 1),
        ring(sent[1], LON, -1),
        passed_along(sent[2], LAT, 1),
        passed_along(sent[3], LAT, -1),
    ]
    place = jnp.stack([edge_count[0, 0], lax.axis_index("lat_1").astype(jnp.int32)])
    new_nodes, new_edges, gz, gagg, node_part, *rest = layer(
        place,
        snd,
        rcv,
        long_need.reshape(1, FAR),
        edges_l,
        ecot,
        nodes_l,
        halo,
        far,
        node_cot[0, 0],
        e_w1,
        e_w2,
        n_w1,
        n_w2,
        e_b1,
        e_gain,
        n_b1,
        n_gain,
    )
    halo_grad, (keep, send) = rest[:4], rest[4:]
    pair = lax.ppermute(send, "lat_1", [(0, 1), (1, 0)])
    both = (keep.astype(F32) + pair.astype(F32)).astype(BF).reshape(64, GROUP_ROWS // 4, WIDE)
    both, halo_grad, gz = lax.optimization_barrier((both, halo_grad, gz))
    parts = lax.all_to_all(
        both, ("lat_0", "lon_0", "lon_1"), split_axis=0, concat_axis=0, tiled=True
    )
    edge_grad = edge_grads(place, rcv, ecot, gz, gagg, e_w1)
    returned = [
        ring(halo_grad[0], LON, -1),
        ring(halo_grad[1], LON, 1),
        passed_along(halo_grad[2], LAT, -1),
        passed_along(halo_grad[3], LAT, 1),
    ]
    border = (rows_out.reshape(1, 4 * HALO) == lax.broadcasted_iota(jnp.int32, (NODES, 4 * HALO), 0)).astype(BF)
    node_grad = node_part + jnp.dot(border, jnp.concatenate(returned, axis=0), preferred_element_type=F32)
    parts, edge_grad, node_grad = lax.optimization_barrier((parts, edge_grad, node_grad))
    lane = ((lax.axis_index(LAT_LON) & 63) * 4).astype(jnp.int32).reshape(1)
    node_grad, *sums = finish(lane, jnp.sum(parts.astype(F32), axis=0), node_grad)
    return (
        new_nodes[None, None],
        new_edges[None, None],
        node_grad[None, None],
        edge_grad[None, None],
        *sums,
    )


def solution(mesh):
    finer = Mesh(mesh.devices.reshape(4, 2, 4, 4), ("lat_0", "lat_1", "lon_0", "lon_1"))
    placed = (
        P(LAT, LON, None, None),
        P(LAT, LON, None, None),
        P(LAT, LON, None),
        P(LAT, LON, None),
        P(LAT, LON),
        P(LAT, LON, None, None),
        P(LAT, LON, None, None),
        P(LAT, LON, None, None),
        P(LAT, LON, None, None),
        P(),
        P(),
        P(),
        P(),
        P(),
        P(),
        P(),
        P(),
    )
    return jax.shard_map(
        shards,
        mesh=finer,
        in_specs=placed,
        out_specs=(
            P(LAT, LON, None, None),
            P(LAT, LON, None, None),
            P(LAT, LON, None, None),
            P(LAT, LON, None, None),
            P(LAT_LON, None),
            P(LAT_LON),
            P(LAT_LON, None),
            P(LAT_LON),
            P(LAT_LON, None),
            P(LAT_LON),
            P(LAT_LON, None),
            P(LAT_LON),
        ),
        check_vma=False,
    )
```

```python
import functools

import jax
import jax.numpy as jnp
from jax import lax
from jax.experimental import pallas as pl
from jax.experimental.pallas import tpu as pltpu
from jax.sharding import Mesh
from jax.sharding import PartitionSpec as P

COARSE = 2
LON = ("lon_0", "lon_1")
LAT = ("lat_0", "lat_1")
LAT_LON = ("lat_0", "lat_1", "lon_0", "lon_1")
EPS = 1e-05
BF = jnp.bfloat16
F32 = jnp.float32

NODES = 384
HALO = 24
WIDE = 512
EDGES = 3072
FAR = 128
BLOCK = 1024
STEPS = EDGES // BLOCK
SENDERS = 640
ONES_ROW = 608
TABLE = SENDERS + NODES
FIRST = WIDE + SENDERS
GROUPS = 32
GROUP_ROWS = 128


def mm(a, b):
    return lax.dot_general(a, b, (((1,), (0,)), ((), ())), preferred_element_type=F32)


def mm_t(a, b):
    return lax.dot_general(a, b, (((1,), (1,)), ((), ())), preferred_element_type=F32)


def t_mm(a, b):
    return lax.dot_general(a, b, (((0,), (0,)), ((), ())), preferred_element_type=F32)


def row_mean(v):
    return jnp.sum(v, axis=1, keepdims=True) * (1.0 / WIDE)


def first_act(z):
    sig = 0.5 + 0.5 * jnp.tanh(0.5 * z)
    act = z * sig
    return act, sig + act * (1.0 - sig)


def normalise(z):
    centred = z - row_mean(z)
    rstd = lax.rsqrt(row_mean(centred * centred) + EPS)
    return centred * rstd, rstd


def norm_back(g, normed, rstd, gain):
    s = g * gain
    return rstd * (s - row_mean(s) - normed * row_mean(s * normed))


def lane_ids(row):
    return jnp.transpose(jnp.broadcast_to(row, (128, BLOCK)))


def hot_lanes(ids, first, chunks):
    lane = lax.broadcasted_iota(jnp.int32, (BLOCK, 128), 1).astype(F32)
    return [
        jnp.where(ids == lane + float(first + 128 * j), 1.0, 0.0).astype(BF) for j in range(chunks)
    ]


def spread_kernel(nodes_ref, coarse_ref):
    coarse_ref[...] = jnp.broadcast_to(nodes_ref[0:COARSE][None], (FAR, COARSE, WIDE))


def spread(nodes):
    return pl.pallas_call(
        spread_kernel,
        name="spread_coarse",
        grid=(1,),
        in_specs=[pl.BlockSpec((16, WIDE), lambda i: (0, 0))],
        out_specs=pl.BlockSpec((FAR, COARSE, WIDE), lambda i: (0, 0, 0)),
        out_shape=jax.ShapeDtypeStruct((FAR, COARSE, WIDE), BF),
    )(nodes)


def border_kernel(place_ref, nodes_ref, rows_ref, *sent_refs):
    at = lax.broadcasted_iota(jnp.int32, (NODES, HALO), 0)
    for k, sent_ref in enumerate(sent_refs):
        first = 2 * (k // 2)
        odd = place_ref[2 - k // 2] != 0
        one, two = rows_ref[first + k % 2], rows_ref[first + 1 - k % 2]
        hot = jnp.where(at == jnp.where(odd, two, one).reshape(1, HALO), 1.0, 0.0).astype(BF)
        sent_ref[...] = t_mm(hot, nodes_ref[...]).astype(BF)


def borders(place, nodes, rows_out):
    vmem = pl.BlockSpec(memory_space=pltpu.VMEM)
    return pl.pallas_call(
        border_kernel,
        name="border_rows",
        in_specs=[pl.BlockSpec(memory_space=pltpu.SMEM), vmem, vmem],
        out_shape=[jax.ShapeDtypeStruct((HALO, WIDE), BF)] * 4,
        cost_estimate=pl.CostEstimate(
            flops=8 << 30, transcendentals=0, bytes_accessed=8 << 20
        ),
    )(place, nodes, rows_out)


def whole(*shape):
    return pl.BlockSpec(shape, lambda i: (0,) * len(shape), pipeline_mode=pl.Buffered(1))


def by_block(shape, pick):
    return pl.BlockSpec(shape, lambda i: (pick(i),) + (0,) * (len(shape) - 1))


def params():
    return pltpu.CompilerParams(
        dimension_semantics=("arbitrary",), vmem_limit_bytes=60 * 1024 * 1024
    )


def layer_kernel(
    place_ref,
    snd_ref,
    rcv_ref,
    need_ref,
    lon_a_ref,
    lon_b_ref,
    lat_a_ref,
    lat_b_ref,
    far_ref,
    eb1_ref,
    eg_ref,
    nb1_ref,
    ng_ref,
    edges_hbm,
    ecot_hbm,
    nodes_hbm,
    ncot_hbm,
    ew1_hbm,
    ew2_hbm,
    nw1_hbm,
    nw2_hbm,
    east_ref,
    west_ref,
    north_ref,
    south_ref,
    new_nodes_hbm,
    new_edges_hbm,
    gz_hbm,
    gagg_hbm,
    node_hbm,
    keep_hbm,
    send_hbm,
    nodes_ref,
    ncot_ref,
    ew1_ref,
    ew2_ref,
    nw1_ref,
    nw2_ref,
    table_s,
    right_s,
    left_s,
    ecot_s,
    fresh_s,
    act_s,
    dact_s,
    normed_s,
    rstd_s,
    new_nodes_s,
    gagg_s,
    node_s,
    agg_s,
    dw1_s,
    dw2_s,
    gain_s,
    packed_s,
    whole_sem,
    edges_sem,
    ecot_sem,
    fresh_sem,
    gz_sem,
    packed_sem,
):
    count = place_ref[0]
    egain = eg_ref[...].reshape(1, WIDE)

    def rows_of(i):
        return pl.ds(pl.multiple_of(i * BLOCK, BLOCK), BLOCK)

    def fetch(k):
        pairs = (
            (nodes_hbm, nodes_ref),
            (ew1_hbm, ew1_ref),
            (ew2_hbm, ew2_ref),
            (nw1_hbm, nw1_ref),
            (nw2_hbm, nw2_ref),
            (ncot_hbm, ncot_ref),
        )
        return pltpu.make_async_copy(*pairs[k], whole_sem.at[k])

    def give(k):
        pairs = ((new_nodes_s, new_nodes_hbm), (gagg_s, gagg_hbm), (node_s, node_hbm))
        return pltpu.make_async_copy(*pairs[k], whole_sem.at[6 + k])

    def edges_in(i):
        here = rows_of(i)
        return pltpu.make_async_copy(edges_hbm.at[here], left_s.at[here, 0:WIDE], edges_sem.at[i])

    def ecot_in(i):
        here = rows_of(i)
        return pltpu.make_async_copy(ecot_hbm.at[here], ecot_s.at[here], ecot_sem.at[i])

    def fresh_out(i):
        here = rows_of(i)
        return pltpu.make_async_copy(fresh_s.at[here], new_edges_hbm.at[here], fresh_sem.at[i])

    def gz_out(i):
        here = rows_of(i)
        return pltpu.make_async_copy(ecot_s.at[here], gz_hbm.at[here], gz_sem.at[i])

    def packed_out(g):
        copies = []
        for other, ref in ((0, keep_hbm), (1, send_hbm)):
            group = (g >> 2) * 8 + (place_ref[1] ^ other) * 4 + (g & 3)
            copies.append(
                pltpu.make_async_copy(packed_s.at[group], ref.at[g], packed_sem.at[2 * g + other])
            )
        return copies

    fetch(0).start()
    fetch(1).start()
    edges_in(0).start()
    fetch(2).start()
    for i in range(1, STEPS):
        edges_in(i).start()
    for k in range(3, 6):
        fetch(k).start()
    for i in range(STEPS):
        ecot_in(i).start()

    agg_s[...] = jnp.zeros_like(agg_s)
    dw1_s[...] = jnp.zeros_like(dw1_s)
    dw2_s[...] = jnp.zeros_like(dw2_s)
    gain_s[...] = jnp.zeros_like(gain_s)
    odd_lat, odd_lon = place_ref[1] != 0, place_ref[2] != 0
    lon_a, lon_b, lat_a, lat_b = (
        ref[...].astype(F32) for ref in (lon_a_ref, lon_b_ref, lat_a_ref, lat_b_ref)
    )
    table_s[NODES : NODES + 96] = jnp.concatenate(
        [
            jnp.where(odd_lon, lon_a, lon_b),
            jnp.where(odd_lon, lon_b, lon_a),
            jnp.where(odd_lat, lat_a, lat_b),
            jnp.where(odd_lat, lat_b, lat_a),
        ],
        axis=0,
    ).astype(BF)
    pick = jnp.transpose(jnp.broadcast_to(need_ref[...].astype(F32), (128, 128)))[:, 0:1]
    low, high = far_ref[:, 0].astype(F32), far_ref[:, 1].astype(F32)
    table_s[480:608] = jnp.where(pick == 0.0, low, high).astype(BF)
    table_s[608:SENDERS] = jnp.zeros((32, WIDE), BF)
    fetch(0).wait()
    table_s[0:NODES] = nodes_ref[...]
    fetch(1).wait()
    right_s[0:WIDE] = ew1_ref[0:WIDE]
    right_s[WIDE:FIRST] = mm(table_s[...], ew1_ref[WIDE : 2 * WIDE]).astype(BF)
    right_s[FIRST:] = mm(nodes_ref[...], ew1_ref[2 * WIDE :]).astype(BF)
    fetch(2).wait()

    def forward(i, carry):
        here = rows_of(i)
        at = i * BLOCK
        slot = lax.broadcasted_iota(jnp.int32, (1, BLOCK), 1) + at
        snd = snd_ref[i].astype(F32)
        rcv = jnp.where(slot < count, rcv_ref[i].astype(F32), -1.0)
        hots = hot_lanes(lane_ids(snd), 0, SENDERS // 128)
        lane = lax.broadcasted_iota(jnp.int32, (BLOCK, 128), 1)
        hots[4] = jnp.where(lane == ONES_ROW - 512, 1.0, hots[4].astype(F32)).astype(BF)
        hots += hot_lanes(lane_ids(rcv), 0, NODES // 128)
        for k, hot in enumerate(hots):
            left_s[here, WIDE + 128 * k : WIDE + 128 * (k + 1)] = hot
        edges_in(i).wait()
        z1 = mm(left_s[here], right_s[...]) + eb1_ref[...].reshape(1, WIDE)
        act, dact = first_act(z1)
        act = act.astype(BF)
        act_s[here] = act
        dact_s[here] = dact.astype(BF)
        normed, rstd = normalise(mm(act, ew2_ref[...]))
        normed_s[here] = normed.astype(BF)
        rstd_s[here] = jnp.broadcast_to(rstd, (BLOCK, 128))
        live = (lax.broadcasted_iota(jnp.int32, (BLOCK, 1), 0) + at < count).astype(F32)
        fresh = (left_s[here, 0:WIDE].astype(F32) + (live * normed) * egain).astype(BF)
        fresh_s[here] = fresh
        fresh_out(i).start()
        agg_s[...] += t_mm(left_s[here, FIRST:], fresh)
        return carry

    lax.fori_loop(0, STEPS, forward, 0)

    for k in range(3, 6):
        fetch(k).wait()
    nodes = nodes_ref[...]
    ngain = ng_ref[...].reshape(1, WIDE)
    agg = agg_s[...].astype(BF)
    z1 = mm(nodes, nw1_ref[0:WIDE]) + mm(agg, nw1_ref[WIDE:]) + nb1_ref[...].reshape(1, WIDE)
    act, dact = first_act(z1)
    act = act.astype(BF)
    normed, rstd = normalise(mm(act, nw2_ref[...]))
    new_nodes_s[...] = (nodes.astype(F32) + normed * ngain).astype(BF)
    give(0).start()
    cot = ncot_ref[...].astype(F32)
    gz2 = norm_back(cot, normed, rstd, ngain).astype(BF)
    gain_grad = jnp.sum(cot * normed, axis=0, keepdims=True)
    gz1 = (mm_t(gz2, nw2_ref[...]) * dact).astype(BF)
    bias_grad = jnp.sum(gz1.astype(F32), axis=0, keepdims=True)
    gagg_s[...] = mm_t(gz1, nw1_ref[WIDE:]).astype(BF)
    give(1).start()
    node_s[...] = cot + mm_t(gz1, nw1_ref[0:WIDE])
    packed_s[0:16, 0:32] = t_mm(nodes, gz1).astype(BF).reshape(16, 32, WIDE)
    packed_s[16:32, 0:32] = t_mm(agg, gz1).astype(BF).reshape(16, 32, WIDE)
    packed_s[:, 32:48] = t_mm(act, gz2).astype(BF).reshape(GROUPS, 16, WIDE)

    def backward(i, carry):
        here = rows_of(i)
        live = (lax.broadcasted_iota(jnp.int32, (BLOCK, 1), 0) + i * BLOCK < count).astype(F32)
        ecot_in(i).wait()
        g = live * ecot_s[here].astype(F32) + mm(left_s[here, FIRST:], gagg_s[...])
        normed = normed_s[here].astype(F32)
        gain_s[...] += jnp.sum((g * normed).reshape(BLOCK // 8, 8, WIDE), axis=0)
        gz2 = norm_back(g, normed, rstd_s[here][:, 0:1], egain).astype(BF)
        dw2_s[...] += t_mm(act_s[here], gz2)
        gz1 = (mm_t(gz2, ew2_ref[...]) * dact_s[here].astype(F32)).astype(BF)
        ecot_s[here] = gz1
        gz_out(i).start()
        dw1_s[...] += t_mm(left_s[here], gz1)
        return carry

    lax.fori_loop(0, STEPS, backward, 0)

    sent, got = dw1_s[WIDE:FIRST].astype(BF), dw1_s[FIRST:].astype(BF)
    back = mm_t(sent, ew1_ref[WIDE : 2 * WIDE])
    node_s[...] += back[0:NODES] + mm_t(got, ew1_ref[2 * WIDE :])
    give(2).start()
    packed_s[:, 96:112] = dw2_s[...].astype(BF).reshape(GROUPS, 16, WIDE)
    first = jnp.concatenate(
        [
            dw1_s[0:WIDE].astype(BF),
            t_mm(table_s[...], sent).astype(BF),
            t_mm(nodes, got).astype(BF),
        ],
        axis=0,
    )
    packed_s[:, 48:96] = first.reshape(GROUPS, 48, WIDE)
    for k, ref in enumerate((east_ref, west_ref, north_ref, south_ref)):
        ref[...] = back[NODES + HALO * k : NODES + HALO * (k + 1)].astype(BF)
    vectors = (
        dw1_s[WIDE + ONES_ROW : WIDE + ONES_ROW + 1],
        jnp.sum(gain_s[...], axis=0, keepdims=True),
        bias_grad,
        gain_grad,
    )
    half = WIDE // 2
    paired = [
        jnp.concatenate([vectors[k][:, side], vectors[k + 1][:, side]], axis=1)
        for side in (slice(0, half), slice(half, WIDE))
        for k in (0, 2)
    ]
    extra = jnp.concatenate([back[480:608]] + paired + [jnp.zeros((124, WIDE), F32)], axis=0)
    out = lax.broadcasted_iota(jnp.int32, (GROUPS * 16, 256), 0)
    src = lax.broadcasted_iota(jnp.int32, (GROUPS * 16, 256), 1)
    need = jnp.concatenate([need_ref[...], jnp.zeros((1, 128), jnp.int32)], axis=1)
    slot = out & 15
    low = (slot < 4) & (src == (out >> 4) * 4 + slot) & (need == 0)
    high = (slot >= 4) & (slot < 8) & (src == (out >> 4) * 4 + slot - 4) & (need == 1)
    small = (slot >= 8) & (slot < 10) & (src == 120 + slot + (out >> 8) * 2)
    move = jnp.where(low | high | small, 1.0, 0.0).astype(BF)
    packed_s[:, 112:128] = mm(move, extra.astype(BF)).astype(BF).reshape(GROUPS, 16, WIDE)
    out = lax.broadcasted_iota(jnp.int32, (128, 128), 0)
    src = lax.broadcasted_iota(jnp.int32, (128, 128), 1)
    z, slot = out >> 5, out & 31
    want = jnp.where(slot < 8, 8 * z + slot, 24 + 4 * z + slot)
    want = jnp.where(slot >= 12, 36 + 12 * z + slot, want)
    want = jnp.where(slot >= 24, 72 + 4 * z + slot, want)
    want = jnp.where(slot >= 28, 112 + z + 4 * (slot - 28), want)
    want = jnp.where(slot >= 30, 90 + slot, want)
    order = jnp.where(src == want, 1.0, 0.0).astype(BF)
    for g in range(16):
        for group in ((g >> 2) * 8 + (g & 3), (g >> 2) * 8 + 4 + (g & 3)):
            packed_s[group] = mm(order, packed_s[group]).astype(BF)
        for copy in packed_out(g):
            copy.start()
    for k in range(3):
        give(k).wait()
    for i in range(STEPS):
        fresh_out(i).wait()
        gz_out(i).wait()
    for g in range(16):
        for copy in packed_out(g):
            copy.wait()


def layer(place, snd, rcv, need, edges, ecot, nodes, borders, far, ncot, ew1, ew2, nw1, nw2, eb1, eg, nb1, ng):
    sds = jax.ShapeDtypeStruct
    vmem = pl.BlockSpec(memory_space=pltpu.VMEM)
    hbm = pl.BlockSpec(memory_space=pl.ANY)
    return pl.pallas_call(
        layer_kernel,
        name="mesh_layer",
        in_specs=[pl.BlockSpec(memory_space=pltpu.SMEM)] + [vmem] * 12 + [hbm] * 8,
        out_specs=[vmem] * 4 + [hbm] * 7,
        out_shape=[sds((HALO, WIDE), BF)] * 4
        + [
            sds((NODES, WIDE), BF),
            sds((EDGES, WIDE), BF),
            sds((EDGES, WIDE), BF),
            sds((NODES, WIDE), BF),
            sds((NODES, WIDE), F32),
        ]
        + [sds((16, GROUP_ROWS, WIDE), BF)] * 2,
        scratch_shapes=[
            pltpu.VMEM((NODES, WIDE), BF),
            pltpu.VMEM((NODES, WIDE), BF),
            pltpu.VMEM((3 * WIDE, WIDE), BF),
            pltpu.VMEM((WIDE, WIDE), BF),
            pltpu.VMEM((2 * WIDE, WIDE), BF),
            pltpu.VMEM((WIDE, WIDE), BF),
            pltpu.VMEM((SENDERS, WIDE), BF),
            pltpu.VMEM((WIDE + TABLE, WIDE), BF),
            pltpu.VMEM((EDGES, WIDE + TABLE), BF),
            pltpu.VMEM((EDGES, WIDE), BF),
            pltpu.VMEM((EDGES, WIDE), BF),
            pltpu.VMEM((EDGES, WIDE), BF),
            pltpu.VMEM((EDGES, WIDE), BF),
            pltpu.VMEM((EDGES, WIDE), BF),
            pltpu.VMEM((EDGES, 128), F32),
            pltpu.VMEM((NODES, WIDE), BF),
            pltpu.VMEM((NODES, WIDE), BF),
            pltpu.VMEM((NODES, WIDE), F32),
            pltpu.VMEM((NODES, WIDE), F32),
            pltpu.VMEM((WIDE + TABLE, WIDE), F32),
            pltpu.VMEM((WIDE, WIDE), F32),
            pltpu.VMEM((8, WIDE), F32),
            pltpu.VMEM((GROUPS, GROUP_ROWS, WIDE), BF),
            pltpu.SemaphoreType.DMA((9,)),
            pltpu.SemaphoreType.DMA((STEPS,)),
            pltpu.SemaphoreType.DMA((STEPS,)),
            pltpu.SemaphoreType.DMA((STEPS,)),
            pltpu.SemaphoreType.DMA((STEPS,)),
            pltpu.SemaphoreType.DMA((32,)),
        ],
        compiler_params=pltpu.CompilerParams(vmem_limit_bytes=60 * 1024 * 1024),
        cost_estimate=pl.CostEstimate(
            flops=18 << 30, transcendentals=4 << 20, bytes_accessed=30 << 20
        ),
    )(place, snd, rcv, need, *borders, far, eb1, eg, nb1, ng, edges, ecot, nodes, ncot, ew1, ew2, nw1, nw2)


def edge_grad_kernel(count_ref, rcv_ref, ecot_ref, gz_ref, gagg_ref, ew1_ref, out_ref):
    at = pl.program_id(0) * BLOCK
    back = jnp.concatenate(hot_lanes(lane_ids(rcv_ref[0].astype(F32)), 0, NODES // 128), axis=1)
    live = (lax.broadcasted_iota(jnp.int32, (BLOCK, 1), 0) + at < count_ref[0]).astype(F32)
    taken = live * mm(back, gagg_ref[...])
    out_ref[...] = ecot_ref[...].astype(F32) + taken + mm_t(gz_ref[...], ew1_ref[...])


def edge_grads(place, rcv, ecot, gz, gagg, ew1):
    same = lambda i: i
    return pl.pallas_call(
        edge_grad_kernel,
        name="edge_grads",
        grid=(STEPS,),
        in_specs=[
            pl.BlockSpec(memory_space=pltpu.SMEM),
            by_block((1, 1, BLOCK), same),
            by_block((BLOCK, WIDE), same),
            by_block((BLOCK, WIDE), same),
            whole(NODES, WIDE),
            whole(WIDE, WIDE),
        ],
        out_specs=by_block((BLOCK, WIDE), same),
        out_shape=jax.ShapeDtypeStruct((EDGES, WIDE), F32),
        compiler_params=params(),
        cost_estimate=pl.CostEstimate(
            flops=2 * EDGES * WIDE * (WIDE + NODES), transcendentals=0, bytes_accessed=13 << 20
        ),
    )(place, rcv, ecot, gz, gagg, ew1)


def finish_kernel(lane_ref, total_ref, node_ref, out_ref, *grads):
    total = total_ref[...]
    ew1, eb1, ew2, eg, nw1, nb1, nw2, ng = grads
    nw1[...] = total[0:8]
    nw2[...] = total[8:12]
    ew1[...] = total[12:24]
    ew2[...] = total[24:28]
    out_ref[...] = node_ref[...]
    out_ref[0:COARSE] += total[28:30]
    half = WIDE // 2
    lines = [total[30:31, :half], total[30:31, half:], total[31:32, :half], total[31:32, half:]]
    lines = jnp.concatenate(lines + [jnp.zeros((4, half), F32)], axis=0)
    lines = pltpu.roll(lines, (half - lane_ref[0]) & (half - 1), 1)
    for k, ref in enumerate((eb1, eg, nb1, ng)):
        ref[...] = lines[k, 0:4]


def finish(lane, total, node_grad):
    sds = jax.ShapeDtypeStruct
    rows = [(12, WIDE), (4,), (4, WIDE), (4,), (8, WIDE), (4,), (4, WIDE), (4,)]
    first = pl.BlockSpec((8, WIDE), lambda i: (0, 0))
    return pl.pallas_call(
        finish_kernel,
        name="finish_grads",
        grid=(1,),
        in_specs=[
            pl.BlockSpec(memory_space=pltpu.SMEM),
            whole(GROUP_ROWS // 4, WIDE),
            first,
        ],
        out_specs=[first] + [pl.BlockSpec(r, lambda i, n=len(r): (0,) * n) for r in rows],
        out_shape=[sds((NODES, WIDE), F32)] + [sds(r, F32) for r in rows],
        input_output_aliases={2: 0},
        compiler_params=params(),
    )(lane, total, node_grad)


def ring(block, axis, distance):
    n = lax.axis_size(axis)
    return lax.ppermute(block, axis, [(i, (i + distance) % n) for i in range(n)])


def swap(block, axis, first, around):
    n = lax.axis_size(axis)
    pairs = [(i, (i + 1) % n) for i in range(first, n, 2) if around or i + 1 < n]
    return lax.ppermute(block, axis, pairs + [(j, i) for i, j in pairs])


def passed_along(value, axis, steps):
    count = lax.axis_size(axis)
    leading, last = (max(0, -steps), min(count, count - steps))
    return lax.ppermute(value, axis, [(source, source + steps) for source in range(leading, last)])


def shards(
    nodes,
    edges,
    senders,
    receivers,
    edge_count,
    halo_send,
    long_need,
    node_cot,
    edge_cot,
    e_w1,
    e_b1,
    e_w2,
    e_gain,
    n_w1,
    n_b1,
    n_w2,
    n_gain,
):
    nodes_l, edges_l, ecot = nodes[0, 0], edges[0, 0], edge_cot[0, 0]
    rows_out = halo_send[0, 0]
    snd = senders.reshape(STEPS, 1, BLOCK)
    rcv = receivers.reshape(STEPS, 1, BLOCK)
    far = lax.all_to_all(spread(nodes_l), LAT_LON, split_axis=0, concat_axis=0, tiled=True)
    place = jnp.stack(
        [
            edge_count[0, 0],
            lax.axis_index("lat_1").astype(jnp.int32),
            (lax.axis_index("lon_1") & 1).astype(jnp.int32),
        ]
    )
    sent = borders(place, nodes_l, rows_out)
    halo = [
        swap(sent[0], LON, 0, True),
        swap(sent[1], LON, 1, True),
        swap(sent[2], LAT, 0, False),
        swap(sent[3], LAT, 1, False),
    ]
    *halo_grad, new_nodes, new_edges, gz, gagg, node_part, keep, send = layer(
        place,
        snd,
        rcv,
        long_need.reshape(1, FAR),
        edges_l,
        ecot,
        nodes_l,
        halo,
        far,
        node_cot[0, 0],
        e_w1,
        e_w2,
        n_w1,
        n_w2,
        e_b1,
        e_gain,
        n_b1,
        n_gain,
    )
    pair = lax.ppermute(send, "lat_1", [(0, 1), (1, 0)])
    both = (keep.astype(F32) + pair.astype(F32)).astype(BF).reshape(64, GROUP_ROWS // 4, WIDE)
    both, halo_grad, gz = lax.optimization_barrier((both, halo_grad, gz))
    parts = lax.all_to_all(
        both, ("lat_0", "lon_0", "lon_1"), split_axis=0, concat_axis=0, tiled=True
    )
    edge_grad = edge_grads(place, rcv, ecot, gz, gagg, e_w1)
    returned = [
        ring(halo_grad[0], LON, -1),
        ring(halo_grad[1], LON, 1),
        passed_along(halo_grad[2], LAT, -1),
        passed_along(halo_grad[3], LAT, 1),
    ]
    border = (rows_out.reshape(1, 4 * HALO) == lax.broadcasted_iota(jnp.int32, (NODES, 4 * HALO), 0)).astype(BF)
    node_grad = node_part + jnp.dot(border, jnp.concatenate(returned, axis=0), preferred_element_type=F32)
    parts, edge_grad, node_grad = lax.optimization_barrier((parts, edge_grad, node_grad))
    lane = ((lax.axis_index(LAT_LON) & 63) * 4).astype(jnp.int32).reshape(1)
    node_grad, *sums = finish(lane, jnp.sum(parts.astype(F32), axis=0), node_grad)
    return (
        new_nodes[None, None],
        new_edges[None, None],
        node_grad[None, None],
        edge_grad[None, None],
        *sums,
    )


def solution(mesh):
    finer = Mesh(mesh.devices.reshape(4, 2, 4, 4), ("lat_0", "lat_1", "lon_0", "lon_1"))
    placed = (
        P(LAT, LON, None, None),
        P(LAT, LON, None, None),
        P(LAT, LON, None),
        P(LAT, LON, None),
        P(LAT, LON),
        P(LAT, LON, None, None),
        P(LAT, LON, None, None),
        P(LAT, LON, None, None),
        P(LAT, LON, None, None),
        P(),
        P(),
        P(),
        P(),
        P(),
        P(),
        P(),
        P(),
    )
    return jax.shard_map(
        shards,
        mesh=finer,
        in_specs=placed,
        out_specs=(
            P(LAT, LON, None, None),
            P(LAT, LON, None, None),
            P(LAT, LON, None, None),
            P(LAT, LON, None, None),
            P(LAT_LON, None),
            P(LAT_LON),
            P(LAT_LON, None),
            P(LAT_LON),
            P(LAT_LON, None),
            P(LAT_LON),
            P(LAT_LON, None),
            P(LAT_LON),
        ),
        check_vma=False,
    )
```

```python
import functools

import jax
import jax.numpy as jnp
from jax import lax
from jax.experimental import pallas as pl
from jax.experimental.pallas import tpu as pltpu
from jax.sharding import Mesh
from jax.sharding import PartitionSpec as P

COARSE = 2
LON = ("lon_0", "lon_1")
LAT = ("lat_0", "lat_1")
LAT_LON = ("lat_0", "lat_1", "lon_0", "lon_1")
EPS = 1e-05
BF = jnp.bfloat16
F32 = jnp.float32

NODES = 384
HALO = 24
WIDE = 512
EDGES = 3072
FAR = 128
BLOCK = 1024
STEPS = EDGES // BLOCK
SENDERS = 640
ONES_ROW = 608
TABLE = SENDERS + NODES
FIRST = WIDE + SENDERS
GROUPS = 32
GROUP_ROWS = 128


def mm(a, b):
    return lax.dot_general(a, b, (((1,), (0,)), ((), ())), preferred_element_type=F32)


def mm_t(a, b):
    return lax.dot_general(a, b, (((1,), (1,)), ((), ())), preferred_element_type=F32)


def t_mm(a, b):
    return lax.dot_general(a, b, (((0,), (0,)), ((), ())), preferred_element_type=F32)


def row_mean(v):
    return jnp.sum(v, axis=1, keepdims=True) * (1.0 / WIDE)


def first_act(z):
    sig = 0.5 + 0.5 * jnp.tanh(0.5 * z)
    act = z * sig
    return act, sig + act * (1.0 - sig)


def normalise(z):
    centred = z - row_mean(z)
    rstd = lax.rsqrt(row_mean(centred * centred) + EPS)
    return centred * rstd, rstd


def norm_back(g, normed, rstd, gain):
    s = g * gain
    return rstd * (s - row_mean(s) - normed * row_mean(s * normed))


def lane_ids(row):
    return jnp.transpose(jnp.broadcast_to(row, (128, BLOCK)))


def hot_lanes(ids, first, chunks):
    lane = lax.broadcasted_iota(jnp.int32, (BLOCK, 128), 1).astype(F32)
    return [
        jnp.where(ids == lane + float(first + 128 * j), 1.0, 0.0).astype(BF) for j in range(chunks)
    ]


def border_kernel(place_ref, nodes_ref, rows_ref, *sent_refs):
    at = lax.broadcasted_iota(jnp.int32, (NODES, HALO), 0)
    for k, sent_ref in enumerate(sent_refs):
        first = 2 * (k // 2)
        odd = place_ref[2 - k // 2] != 0
        one, two = rows_ref[first + k % 2], rows_ref[first + 1 - k % 2]
        hot = jnp.where(at == jnp.where(odd, two, one).reshape(1, HALO), 1.0, 0.0).astype(BF)
        sent_ref[...] = t_mm(hot, nodes_ref[...]).astype(BF)


def borders(place, nodes, rows_out):
    vmem = pl.BlockSpec(memory_space=pltpu.VMEM)
    return pl.pallas_call(
        border_kernel,
        name="border_rows",
        in_specs=[pl.BlockSpec(memory_space=pltpu.SMEM), vmem, vmem],
        out_shape=[jax.ShapeDtypeStruct((HALO, WIDE), BF)] * 4,
        cost_estimate=pl.CostEstimate(
            flops=8 << 30, transcendentals=0, bytes_accessed=8 << 20
        ),
    )(place, nodes, rows_out)


def whole(*shape):
    return pl.BlockSpec(shape, lambda i: (0,) * len(shape), pipeline_mode=pl.Buffered(1))


def by_block(shape, pick):
    return pl.BlockSpec(shape, lambda i: (pick(i),) + (0,) * (len(shape) - 1))


def params():
    return pltpu.CompilerParams(
        dimension_semantics=("arbitrary",), vmem_limit_bytes=60 * 1024 * 1024
    )


def layer_kernel(
    place_ref,
    snd_ref,
    rcv_ref,
    need_ref,
    lon_a_ref,
    lon_b_ref,
    lat_a_ref,
    lat_b_ref,
    far_ref,
    eb1_ref,
    eg_ref,
    nb1_ref,
    ng_ref,
    edges_hbm,
    ecot_hbm,
    nodes_hbm,
    ncot_hbm,
    ew1_hbm,
    ew2_hbm,
    nw1_hbm,
    nw2_hbm,
    east_ref,
    west_ref,
    north_ref,
    south_ref,
    new_nodes_hbm,
    new_edges_hbm,
    gz_hbm,
    gagg_hbm,
    node_hbm,
    keep_hbm,
    send_hbm,
    nodes_ref,
    ncot_ref,
    ew1_ref,
    ew2_ref,
    nw1_ref,
    nw2_ref,
    table_s,
    right_s,
    left_s,
    ecot_s,
    fresh_s,
    act_s,
    dact_s,
    normed_s,
    rstd_s,
    new_nodes_s,
    gagg_s,
    node_s,
    agg_s,
    dw1_s,
    dw2_s,
    gain_s,
    packed_s,
    half_s,
    whole_sem,
    edges_sem,
    ecot_sem,
    fresh_sem,
    gz_sem,
    packed_sem,
):
    count = place_ref[0]
    egain = eg_ref[...].reshape(1, WIDE)

    def rows_of(i):
        return pl.ds(pl.multiple_of(i * BLOCK, BLOCK), BLOCK)

    def fetch(k):
        pairs = (
            (nodes_hbm, nodes_ref),
            (ew1_hbm, ew1_ref),
            (ew2_hbm, ew2_ref),
            (nw1_hbm, nw1_ref),
            (nw2_hbm, nw2_ref),
            (ncot_hbm, ncot_ref),
        )
        return pltpu.make_async_copy(*pairs[k], whole_sem.at[k])

    def give(k):
        pairs = ((new_nodes_s, new_nodes_hbm), (gagg_s, gagg_hbm), (node_s, node_hbm))
        return pltpu.make_async_copy(*pairs[k], whole_sem.at[6 + k])

    def edges_in(i):
        here = rows_of(i)
        return pltpu.make_async_copy(edges_hbm.at[here], left_s.at[here, 0:WIDE], edges_sem.at[i])

    def ecot_in(i):
        here = rows_of(i)
        return pltpu.make_async_copy(ecot_hbm.at[here], ecot_s.at[here], ecot_sem.at[i])

    def fresh_out(i):
        here = rows_of(i)
        return pltpu.make_async_copy(fresh_s.at[here], new_edges_hbm.at[here], fresh_sem.at[i])

    def gz_out(i):
        here = rows_of(i)
        return pltpu.make_async_copy(ecot_s.at[here], gz_hbm.at[here], gz_sem.at[i])

    def packed_out(g, half):
        copies = []
        for other, ref in ((0, keep_hbm), (1, send_hbm)):
            group = (g >> 2) * 8 + (place_ref[1] ^ other) * 4 + (g & 3)
            part = slice(16 * half, 16 * (half + 1))
            copies.append(
                pltpu.make_async_copy(
                    packed_s.at[group, :, part],
                    ref.at[g, :, part],
                    packed_sem.at[4 * g + 2 * other + half],
                )
            )
        return copies

    def pack(half, want):
        out = lax.broadcasted_iota(jnp.int32, (64, 64), 0)
        src = lax.broadcasted_iota(jnp.int32, (64, 64), 1)
        order = jnp.where(src == want(out >> 4, out & 15), 1.0, 0.0).astype(BF)
        part = slice(16 * half, 16 * (half + 1))
        for g in range(16):
            for group in ((g >> 2) * 8 + (g & 3), (g >> 2) * 8 + 4 + (g & 3)):
                rows = packed_s[group, :, part].reshape(64, WIDE)
                packed_s[group, :, part] = mm(order, rows).astype(BF).reshape(4, 16, WIDE)
            for copy in packed_out(g, half):
                copy.start()

    fetch(0).start()
    fetch(1).start()
    edges_in(0).start()
    fetch(2).start()
    for i in range(1, STEPS):
        edges_in(i).start()
    for k in range(3, 6):
        fetch(k).start()
    for i in range(STEPS):
        ecot_in(i).start()

    agg_s[...] = jnp.zeros_like(agg_s)
    dw1_s[...] = jnp.zeros_like(dw1_s)
    dw2_s[...] = jnp.zeros_like(dw2_s)
    gain_s[...] = jnp.zeros_like(gain_s)
    odd_lat, odd_lon = place_ref[1] != 0, place_ref[2] != 0
    lon_a, lon_b, lat_a, lat_b = (
        ref[...].astype(F32) for ref in (lon_a_ref, lon_b_ref, lat_a_ref, lat_b_ref)
    )
    table_s[NODES : NODES + 96] = jnp.concatenate(
        [
            jnp.where(odd_lon, lon_a, lon_b),
            jnp.where(odd_lon, lon_b, lon_a),
            jnp.where(odd_lat, lat_a, lat_b),
            jnp.where(odd_lat, lat_b, lat_a),
        ],
        axis=0,
    ).astype(BF)
    pick = jnp.transpose(jnp.broadcast_to(need_ref[...].astype(F32), (128, 128)))[:, 0:1]
    low, high = far_ref[:, 0].astype(F32), far_ref[:, 1].astype(F32)
    table_s[480:608] = jnp.where(pick == 0.0, low, high).astype(BF)
    table_s[608:SENDERS] = jnp.zeros((32, WIDE), BF)
    fetch(0).wait()
    table_s[0:NODES] = nodes_ref[...]
    fetch(1).wait()
    right_s[0:WIDE] = (ew1_ref[0:WIDE].astype(F32) * 0.5).astype(BF)
    right_s[WIDE : WIDE + ONES_ROW] = (
        mm(table_s[0:ONES_ROW], ew1_ref[WIDE : 2 * WIDE]) * 0.5
    ).astype(BF)
    bias = eb1_ref[...].reshape(1, WIDE) * 0.5
    coarse = bias.astype(BF).astype(F32)
    right_s[WIDE + ONES_ROW : FIRST] = jnp.concatenate(
        [coarse, bias - coarse, jnp.zeros((30, WIDE), F32)], axis=0
    ).astype(BF)
    right_s[FIRST:] = (mm(nodes_ref[...], ew1_ref[2 * WIDE :]) * 0.5).astype(BF)
    fetch(2).wait()
    half_s[...] = (ew2_ref[...].astype(F32) * 0.5).astype(BF)

    def forward(i, carry):
        here = rows_of(i)
        at = i * BLOCK
        slot = lax.broadcasted_iota(jnp.int32, (1, BLOCK), 1) + at
        snd = snd_ref[i].astype(F32)
        rcv = jnp.where(slot < count, rcv_ref[i].astype(F32), -1.0)
        hots = hot_lanes(lane_ids(snd), 0, SENDERS // 128)
        lane = lax.broadcasted_iota(jnp.int32, (BLOCK, 128), 1)
        hots[4] = jnp.where((lane == ONES_ROW - 512) | (lane == ONES_ROW - 511), 1.0, hots[4].astype(F32)).astype(BF)
        hots += hot_lanes(lane_ids(rcv), 0, NODES // 128)
        for k, hot in enumerate(hots):
            left_s[here, WIDE + 128 * k : WIDE + 128 * (k + 1)] = hot
        edges_in(i).wait()
        half = mm(left_s[here], right_s[...])
        t = jnp.tanh(half)
        up = 1.0 + t
        act = (half * up).astype(BF)
        act_s[here] = act
        dact_s[here] = (up * (1.0 + half * (1.0 - t))).astype(BF)
        live = lax.broadcasted_iota(jnp.int32, (BLOCK, 1), 0) + at < count
        z2 = mm(act, ew2_ref[...])
        centred = z2 - row_mean(z2)
        rstd = jnp.where(live, lax.rsqrt(row_mean(centred * centred) + EPS), 0.0)
        normed = centred * rstd
        normed_s[here] = normed.astype(BF)
        rstd_s[here] = jnp.broadcast_to(rstd, (BLOCK, 128))
        fresh = (left_s[here, 0:WIDE].astype(F32) + normed * egain).astype(BF)
        fresh_s[here] = fresh
        fresh_out(i).start()
        agg_s[...] += t_mm(left_s[here, FIRST:], fresh)
        return carry

    lax.fori_loop(0, STEPS, forward, 0)

    for k in range(3, 6):
        fetch(k).wait()
    nodes = nodes_ref[...]
    ngain = ng_ref[...].reshape(1, WIDE)
    agg = agg_s[...].astype(BF)
    z1 = mm(nodes, nw1_ref[0:WIDE]) + mm(agg, nw1_ref[WIDE:]) + nb1_ref[...].reshape(1, WIDE)
    act, dact = first_act(z1)
    act = act.astype(BF)
    normed, rstd = normalise(mm(act, nw2_ref[...]))
    new_nodes_s[...] = (nodes.astype(F32) + normed * ngain).astype(BF)
    give(0).start()
    cot = ncot_ref[...].astype(F32)
    gz2 = norm_back(cot, normed, rstd, ngain).astype(BF)
    gain_grad = jnp.sum(cot * normed, axis=0, keepdims=True)
    gz1 = (mm_t(gz2, nw2_ref[...]) * dact).astype(BF)
    bias_grad = jnp.sum(gz1.astype(F32), axis=0, keepdims=True)
    gagg_s[...] = mm_t(gz1, nw1_ref[WIDE:]).astype(BF)
    give(1).start()
    node_s[...] = cot + mm_t(gz1, nw1_ref[0:WIDE])
    packed_s[0:16, 0:2, 0:16] = t_mm(nodes, gz1).astype(BF).reshape(16, 2, 16, WIDE)
    packed_s[16:32, 0:2, 0:16] = t_mm(agg, gz1).astype(BF).reshape(16, 2, 16, WIDE)
    packed_s[:, 2, 0:16] = t_mm(act, gz2).astype(BF).reshape(GROUPS, 16, WIDE)

    def backward(i, carry):
        here = rows_of(i)
        ecot_in(i).wait()
        g = ecot_s[here].astype(F32) + mm(left_s[here, FIRST:], gagg_s[...])
        normed = normed_s[here].astype(F32)
        gain_s[...] += jnp.sum((g * normed).reshape(BLOCK // 8, 8, WIDE), axis=0)
        gz2 = norm_back(g, normed, rstd_s[here][:, 0:1], egain).astype(BF)
        dw2_s[...] += t_mm(act_s[here], gz2)
        gz1 = (mm_t(gz2, half_s[...]) * dact_s[here].astype(F32)).astype(BF)
        ecot_s[here] = gz1
        gz_out(i).start()
        dw1_s[...] += t_mm(left_s[here], gz1)
        return carry

    lax.fori_loop(0, STEPS, backward, 0)

    packed_s[:, 3, 0:16] = dw2_s[...].astype(BF).reshape(GROUPS, 16, WIDE)
    pack(
        0,
        lambda z, slot: jnp.where(
            slot < 8, 8 * z + slot, jnp.where(slot < 12, 24 + 4 * z + slot, 36 + 4 * z + slot)
        ),
    )
    sent, got = dw1_s[WIDE:FIRST].astype(BF), dw1_s[FIRST:].astype(BF)
    back = mm_t(sent, ew1_ref[WIDE : 2 * WIDE])
    node_s[...] += back[0:NODES] + mm_t(got, ew1_ref[2 * WIDE :])
    give(2).start()
    first = jnp.concatenate(
        [
            dw1_s[0:WIDE].astype(BF),
            t_mm(table_s[...], sent).astype(BF),
            t_mm(nodes, got).astype(BF),
        ],
        axis=0,
    )
    packed_s[:, 0:3, 16:32] = first.reshape(GROUPS, 3, 16, WIDE)
    for k, ref in enumerate((east_ref, west_ref, north_ref, south_ref)):
        ref[...] = back[NODES + HALO * k : NODES + HALO * (k + 1)].astype(BF)
    vectors = (
        dw1_s[WIDE + ONES_ROW : WIDE + ONES_ROW + 1],
        jnp.sum(gain_s[...], axis=0, keepdims=True),
        bias_grad,
        gain_grad,
    )
    half = WIDE // 2
    paired = [
        jnp.concatenate([vectors[k][:, side], vectors[k + 1][:, side]], axis=1)
        for side in (slice(0, half), slice(half, WIDE))
        for k in (0, 2)
    ]
    extra = jnp.concatenate([back[480:608]] + paired + [jnp.zeros((124, WIDE), F32)], axis=0)
    out = lax.broadcasted_iota(jnp.int32, (GROUPS * 16, 256), 0)
    src = lax.broadcasted_iota(jnp.int32, (GROUPS * 16, 256), 1)
    need = jnp.concatenate([need_ref[...], jnp.zeros((1, 128), jnp.int32)], axis=1)
    slot = out & 15
    low = (slot < 4) & (src == (out >> 4) * 4 + slot) & (need == 0)
    high = (slot >= 4) & (slot < 8) & (src == (out >> 4) * 4 + slot - 4) & (need == 1)
    small = (slot >= 8) & (slot < 10) & (src == 120 + slot + (out >> 8) * 2)
    move = jnp.where(low | high | small, 1.0, 0.0).astype(BF)
    packed_s[:, 3, 16:32] = mm(move, extra.astype(BF)).astype(BF).reshape(GROUPS, 16, WIDE)
    pack(
        1,
        lambda z, slot: jnp.where(
            slot < 12, 12 * z + slot, jnp.where(slot < 14, z + 4 * slot, 42 + slot)
        ),
    )
    for k in range(3):
        give(k).wait()
    for i in range(STEPS):
        fresh_out(i).wait()
        gz_out(i).wait()
    for g in range(16):
        for copy in packed_out(g, 0) + packed_out(g, 1):
            copy.wait()


def layer(place, snd, rcv, need, edges, ecot, nodes, borders, far, ncot, ew1, ew2, nw1, nw2, eb1, eg, nb1, ng):
    sds = jax.ShapeDtypeStruct
    vmem = pl.BlockSpec(memory_space=pltpu.VMEM)
    hbm = pl.BlockSpec(memory_space=pl.ANY)
    return pl.pallas_call(
        layer_kernel,
        name="mesh_layer",
        in_specs=[pl.BlockSpec(memory_space=pltpu.SMEM)] + [vmem] * 12 + [hbm] * 8,
        out_specs=[vmem] * 4 + [hbm] * 7,
        out_shape=[sds((HALO, WIDE), BF)] * 4
        + [
            sds((NODES, WIDE), BF),
            sds((EDGES, WIDE), BF),
            sds((EDGES, WIDE), BF),
            sds((NODES, WIDE), BF),
            sds((NODES, WIDE), F32),
        ]
        + [sds((16, 4, GROUP_ROWS // 4, WIDE), BF)] * 2,
        scratch_shapes=[
            pltpu.VMEM((NODES, WIDE), BF),
            pltpu.VMEM((NODES, WIDE), BF),
            pltpu.VMEM((3 * WIDE, WIDE), BF),
            pltpu.VMEM((WIDE, WIDE), BF),
            pltpu.VMEM((2 * WIDE, WIDE), BF),
            pltpu.VMEM((WIDE, WIDE), BF),
            pltpu.VMEM((SENDERS, WIDE), BF),
            pltpu.VMEM((WIDE + TABLE, WIDE), BF),
            pltpu.VMEM((EDGES, WIDE + TABLE), BF),
            pltpu.VMEM((EDGES, WIDE), BF),
            pltpu.VMEM((EDGES, WIDE), BF),
            pltpu.VMEM((EDGES, WIDE), BF),
            pltpu.VMEM((EDGES, WIDE), BF),
            pltpu.VMEM((EDGES, WIDE), BF),
            pltpu.VMEM((EDGES, 128), F32),
            pltpu.VMEM((NODES, WIDE), BF),
            pltpu.VMEM((NODES, WIDE), BF),
            pltpu.VMEM((NODES, WIDE), F32),
            pltpu.VMEM((NODES, WIDE), F32),
            pltpu.VMEM((WIDE + TABLE, WIDE), F32),
            pltpu.VMEM((WIDE, WIDE), F32),
            pltpu.VMEM((8, WIDE), F32),
            pltpu.VMEM((GROUPS, 4, GROUP_ROWS // 4, WIDE), BF),
            pltpu.VMEM((WIDE, WIDE), BF),
            pltpu.SemaphoreType.DMA((9,)),
            pltpu.SemaphoreType.DMA((STEPS,)),
            pltpu.SemaphoreType.DMA((STEPS,)),
            pltpu.SemaphoreType.DMA((STEPS,)),
            pltpu.SemaphoreType.DMA((STEPS,)),
            pltpu.SemaphoreType.DMA((64,)),
        ],
        compiler_params=pltpu.CompilerParams(vmem_limit_bytes=60 * 1024 * 1024),
        cost_estimate=pl.CostEstimate(
            flops=18 << 30, transcendentals=4 << 20, bytes_accessed=30 << 20
        ),
    )(place, snd, rcv, need, *borders, far, eb1, eg, nb1, ng, edges, ecot, nodes, ncot, ew1, ew2, nw1, nw2)


def edge_grad_kernel(count_ref, rcv_ref, ecot_ref, gz_ref, gagg_ref, ew1_ref, out_ref):
    at = pl.program_id(0) * BLOCK
    back = jnp.concatenate(hot_lanes(lane_ids(rcv_ref[0].astype(F32)), 0, NODES // 128), axis=1)
    live = (lax.broadcasted_iota(jnp.int32, (BLOCK, 1), 0) + at < count_ref[0]).astype(F32)
    taken = live * mm(back, gagg_ref[...])
    out_ref[...] = ecot_ref[...].astype(F32) + taken + mm_t(gz_ref[...], ew1_ref[...])


def edge_grads(place, rcv, ecot, gz, gagg, ew1):
    same = lambda i: i
    return pl.pallas_call(
        edge_grad_kernel,
        name="edge_grads",
        grid=(STEPS,),
        in_specs=[
            pl.BlockSpec(memory_space=pltpu.SMEM),
            by_block((1, 1, BLOCK), same),
            by_block((BLOCK, WIDE), same),
            by_block((BLOCK, WIDE), same),
            whole(NODES, WIDE),
            whole(WIDE, WIDE),
        ],
        out_specs=by_block((BLOCK, WIDE), same),
        out_shape=jax.ShapeDtypeStruct((EDGES, WIDE), F32),
        compiler_params=params(),
        cost_estimate=pl.CostEstimate(
            flops=2 * EDGES * WIDE * (WIDE + NODES), transcendentals=0, bytes_accessed=13 << 20
        ),
    )(place, rcv, ecot, gz, gagg, ew1)


def finish_kernel(lane_ref, total_ref, node_ref, out_ref, *grads):
    total = total_ref[...]
    ew1, eb1, ew2, eg, nw1, nb1, nw2, ng = grads
    nw1[...] = total[0:8]
    nw2[...] = total[8:12]
    ew2[...] = total[12:16]
    ew1[...] = total[16:28]
    out_ref[...] = node_ref[...]
    out_ref[0:COARSE] += total[28:30]
    half = WIDE // 2
    lines = [total[30:31, :half], total[30:31, half:], total[31:32, :half], total[31:32, half:]]
    lines = jnp.concatenate(lines + [jnp.zeros((4, half), F32)], axis=0)
    lines = pltpu.roll(lines, (half - lane_ref[0]) & (half - 1), 1)
    for k, ref in enumerate((eb1, eg, nb1, ng)):
        ref[...] = lines[k, 0:4]


def finish(lane, total, node_grad):
    sds = jax.ShapeDtypeStruct
    rows = [(12, WIDE), (4,), (4, WIDE), (4,), (8, WIDE), (4,), (4, WIDE), (4,)]
    first = pl.BlockSpec((8, WIDE), lambda i: (0, 0))
    return pl.pallas_call(
        finish_kernel,
        name="finish_grads",
        grid=(1,),
        in_specs=[
            pl.BlockSpec(memory_space=pltpu.SMEM),
            whole(GROUP_ROWS // 4, WIDE),
            first,
        ],
        out_specs=[first] + [pl.BlockSpec(r, lambda i, n=len(r): (0,) * n) for r in rows],
        out_shape=[sds((NODES, WIDE), F32)] + [sds(r, F32) for r in rows],
        input_output_aliases={2: 0},
        compiler_params=params(),
    )(lane, total, node_grad)


def ring(block, axis, distance):
    n = lax.axis_size(axis)
    return lax.ppermute(block, axis, [(i, (i + distance) % n) for i in range(n)])


def swap(block, axis, first, around):
    n = lax.axis_size(axis)
    pairs = [(i, (i + 1) % n) for i in range(first, n, 2) if around or i + 1 < n]
    return lax.ppermute(block, axis, pairs + [(j, i) for i, j in pairs])


def passed_along(value, axis, steps):
    count = lax.axis_size(axis)
    leading, last = (max(0, -steps), min(count, count - steps))
    return lax.ppermute(value, axis, [(source, source + steps) for source in range(leading, last)])


def shards(
    nodes,
    edges,
    senders,
    receivers,
    edge_count,
    halo_send,
    long_need,
    node_cot,
    edge_cot,
    e_w1,
    e_b1,
    e_w2,
    e_gain,
    n_w1,
    n_b1,
    n_w2,
    n_gain,
):
    nodes_l, edges_l, ecot = nodes[0, 0], edges[0, 0], edge_cot[0, 0]
    rows_out = halo_send[0, 0]
    snd = senders.reshape(STEPS, 1, BLOCK)
    rcv = receivers.reshape(STEPS, 1, BLOCK)
    far = lax.all_to_all(
        jnp.broadcast_to(nodes_l[None, :COARSE], (FAR, COARSE, WIDE)), LAT_LON, split_axis=0, concat_axis=0, tiled=True)
    place = jnp.stack(
        [
            edge_count[0, 0],
            lax.axis_index("lat_1").astype(jnp.int32),
            (lax.axis_index("lon_1") & 1).astype(jnp.int32),
        ]
    )
    sent = borders(place, nodes_l, rows_out)
    halo = [
        swap(sent[0], LON, 0, True),
        swap(sent[1], LON, 1, True),
        swap(sent[2], LAT, 0, False),
        swap(sent[3], LAT, 1, False),
    ]
    *halo_grad, new_nodes, new_edges, gz, gagg, node_part, keep, send = layer(
        place,
        snd,
        rcv,
        long_need.reshape(1, FAR),
        edges_l,
        ecot,
        nodes_l,
        halo,
        far,
        node_cot[0, 0],
        e_w1,
        e_w2,
        n_w1,
        n_w2,
        e_b1,
        e_gain,
        n_b1,
        n_gain,
    )
    pair = lax.ppermute(send, "lat_1", [(0, 1), (1, 0)])
    both = (keep.astype(F32) + pair.astype(F32)).astype(BF).reshape(64, GROUP_ROWS // 4, WIDE)
    both, halo_grad, gz = lax.optimization_barrier((both, halo_grad, gz))
    parts = lax.all_to_all(
        both, ("lat_0", "lon_0", "lon_1"), split_axis=0, concat_axis=0, tiled=True
    )
    edge_grad = edge_grads(place, rcv, ecot, gz, gagg, e_w1)
    returned = [
        ring(halo_grad[0], LON, -1),
        ring(halo_grad[1], LON, 1),
        passed_along(halo_grad[2], LAT, -1),
        passed_along(halo_grad[3], LAT, 1),
    ]
    border = (rows_out.reshape(1, 4 * HALO) == lax.broadcasted_iota(jnp.int32, (NODES, 4 * HALO), 0)).astype(BF)
    node_grad = node_part + jnp.dot(border, jnp.concatenate(returned, axis=0), preferred_element_type=F32)
    parts, edge_grad, node_grad = lax.optimization_barrier((parts, edge_grad, node_grad))
    lane = ((lax.axis_index(LAT_LON) & 63) * 4).astype(jnp.int32).reshape(1)
    node_grad, *sums = finish(lane, jnp.sum(parts.astype(F32), axis=0), node_grad)
    return (
        new_nodes[None, None],
        new_edges[None, None],
        node_grad[None, None],
        edge_grad[None, None],
        *sums,
    )


def solution(mesh):
    finer = Mesh(mesh.devices.reshape(4, 2, 4, 4), ("lat_0", "lat_1", "lon_0", "lon_1"))
    placed = (
        P(LAT, LON, None, None),
        P(LAT, LON, None, None),
        P(LAT, LON, None),
        P(LAT, LON, None),
        P(LAT, LON),
        P(LAT, LON, None, None),
        P(LAT, LON, None, None),
        P(LAT, LON, None, None),
        P(LAT, LON, None, None),
        P(),
        P(),
        P(),
        P(),
        P(),
        P(),
        P(),
        P(),
    )
    return jax.shard_map(
        shards,
        mesh=finer,
        in_specs=placed,
        out_specs=(
            P(LAT, LON, None, None),
            P(LAT, LON, None, None),
            P(LAT, LON, None, None),
            P(LAT, LON, None, None),
            P(LAT_LON, None),
            P(LAT_LON),
            P(LAT_LON, None),
            P(LAT_LON),
            P(LAT_LON, None),
            P(LAT_LON),
            P(LAT_LON, None),
            P(LAT_LON),
        ),
        check_vma=False,
    )
```

```python
import functools

import jax
import jax.numpy as jnp
from jax import lax
from jax.experimental import pallas as pl
from jax.experimental.pallas import tpu as pltpu
from jax.sharding import Mesh
from jax.sharding import PartitionSpec as P

COARSE = 2
LON = ("lon_0", "lon_1")
LAT = ("lat_0", "lat_1")
LAT_LON = ("lat_0", "lat_1", "lon_0", "lon_1")
EPS = 1e-05
BF = jnp.bfloat16
F32 = jnp.float32

NODES = 384
HALO = 24
WIDE = 512
EDGES = 3072
FAR = 128
BLOCK = 1024
STEPS = EDGES // BLOCK
SENDERS = 640
ONES_ROW = 608
TABLE = SENDERS + NODES
FIRST = WIDE + SENDERS
GROUPS = 32
GROUP_ROWS = 128


def mm(a, b):
    return lax.dot_general(a, b, (((1,), (0,)), ((), ())), preferred_element_type=F32)


def mm_t(a, b):
    return lax.dot_general(a, b, (((1,), (1,)), ((), ())), preferred_element_type=F32)


def t_mm(a, b):
    return lax.dot_general(a, b, (((0,), (0,)), ((), ())), preferred_element_type=F32)


def row_mean(v):
    return jnp.sum(v, axis=1, keepdims=True) * (1.0 / WIDE)


def first_act(z):
    sig = 0.5 + 0.5 * jnp.tanh(0.5 * z)
    act = z * sig
    return act, sig + act * (1.0 - sig)


def normalise(z):
    centred = z - row_mean(z)
    rstd = lax.rsqrt(row_mean(centred * centred) + EPS)
    return centred * rstd, rstd


def norm_back(g, normed, rstd, gain):
    s = g * gain
    return rstd * (s - row_mean(s) - normed * row_mean(s * normed))


def lane_ids(row):
    return jnp.transpose(jnp.broadcast_to(row, (128, BLOCK)))


def hot_lanes(ids, first, chunks):
    lane = lax.broadcasted_iota(jnp.int32, (BLOCK, 128), 1).astype(F32)
    return [
        jnp.where(ids == lane + float(first + 128 * j), 1.0, 0.0).astype(BF) for j in range(chunks)
    ]


def border_kernel(place_ref, nodes_ref, rows_ref, *sent_refs):
    at = lax.broadcasted_iota(jnp.int32, (NODES, HALO), 0)
    for k, sent_ref in enumerate(sent_refs):
        first = 2 * (k // 2)
        odd = place_ref[2 - k // 2] != 0
        one, two = rows_ref[first + k % 2], rows_ref[first + 1 - k % 2]
        hot = jnp.where(at == jnp.where(odd, two, one).reshape(1, HALO), 1.0, 0.0).astype(BF)
        sent_ref[...] = t_mm(hot, nodes_ref[...]).astype(BF)


def borders(place, nodes, rows_out):
    vmem = pl.BlockSpec(memory_space=pltpu.VMEM)
    return pl.pallas_call(
        border_kernel,
        name="border_rows",
        in_specs=[pl.BlockSpec(memory_space=pltpu.SMEM), vmem, vmem],
        out_shape=[jax.ShapeDtypeStruct((HALO, WIDE), BF)] * 4,
        cost_estimate=pl.CostEstimate(
            flops=8 << 30, transcendentals=0, bytes_accessed=8 << 20
        ),
    )(place, nodes, rows_out)


def whole(*shape):
    return pl.BlockSpec(shape, lambda i: (0,) * len(shape), pipeline_mode=pl.Buffered(1))


def by_block(shape, pick):
    return pl.BlockSpec(shape, lambda i: (pick(i),) + (0,) * (len(shape) - 1))


def params():
    return pltpu.CompilerParams(
        dimension_semantics=("arbitrary",), vmem_limit_bytes=60 * 1024 * 1024
    )


def layer_kernel(
    place_ref,
    snd_ref,
    rcv_ref,
    need_ref,
    lon_a_ref,
    lon_b_ref,
    lat_a_ref,
    lat_b_ref,
    far_ref,
    eb1_ref,
    eg_ref,
    nb1_ref,
    ng_ref,
    edges_hbm,
    ecot_hbm,
    nodes_hbm,
    ncot_hbm,
    ew1_hbm,
    ew2_hbm,
    nw1_hbm,
    nw2_hbm,
    back_lon_a_ref,
    back_lon_b_ref,
    back_lat_a_ref,
    back_lat_b_ref,
    new_nodes_hbm,
    new_edges_hbm,
    gz_hbm,
    gagg_hbm,
    node_hbm,
    keep_hbm,
    send_hbm,
    nodes_ref,
    ncot_ref,
    ew1_ref,
    ew2_ref,
    nw1_ref,
    nw2_ref,
    table_s,
    right_s,
    left_s,
    ecot_s,
    fresh_s,
    act_s,
    dact_s,
    normed_s,
    rstd_s,
    new_nodes_s,
    gagg_s,
    node_s,
    agg_s,
    dw1_s,
    dw2_s,
    gain_s,
    packed_s,
    half_s,
    whole_sem,
    edges_sem,
    ecot_sem,
    fresh_sem,
    gz_sem,
    packed_sem,
):
    count = place_ref[0]
    egain = eg_ref[...].reshape(1, WIDE)

    def rows_of(i):
        return pl.ds(pl.multiple_of(i * BLOCK, BLOCK), BLOCK)

    def fetch(k):
        pairs = (
            (nodes_hbm, nodes_ref),
            (ew1_hbm, ew1_ref),
            (ew2_hbm, ew2_ref),
            (nw1_hbm, nw1_ref),
            (nw2_hbm, nw2_ref),
            (ncot_hbm, ncot_ref),
        )
        return pltpu.make_async_copy(*pairs[k], whole_sem.at[k])

    def give(k):
        pairs = ((new_nodes_s, new_nodes_hbm), (gagg_s, gagg_hbm), (node_s, node_hbm))
        return pltpu.make_async_copy(*pairs[k], whole_sem.at[6 + k])

    def edges_in(i):
        here = rows_of(i)
        return pltpu.make_async_copy(edges_hbm.at[here], left_s.at[here, 0:WIDE], edges_sem.at[i])

    def ecot_in(i):
        here = rows_of(i)
        return pltpu.make_async_copy(ecot_hbm.at[here], ecot_s.at[here], ecot_sem.at[i])

    def fresh_out(i):
        here = rows_of(i)
        return pltpu.make_async_copy(fresh_s.at[here], new_edges_hbm.at[here], fresh_sem.at[i])

    def gz_out(i):
        here = rows_of(i)
        return pltpu.make_async_copy(ecot_s.at[here], gz_hbm.at[here], gz_sem.at[i])

    def packed_out(g, half):
        copies = []
        for other, ref in ((0, keep_hbm), (1, send_hbm)):
            group = (g >> 2) * 8 + (place_ref[1] ^ other) * 4 + (g & 3)
            part = slice(16 * half, 16 * (half + 1))
            copies.append(
                pltpu.make_async_copy(
                    packed_s.at[group, :, part],
                    ref.at[g, :, part],
                    packed_sem.at[4 * g + 2 * other + half],
                )
            )
        return copies

    def pack(half, want):
        out = lax.broadcasted_iota(jnp.int32, (64, 64), 0)
        src = lax.broadcasted_iota(jnp.int32, (64, 64), 1)
        order = jnp.where(src == want(out >> 4, out & 15), 1.0, 0.0).astype(BF)
        part = slice(16 * half, 16 * (half + 1))
        for g in range(16):
            for group in ((g >> 2) * 8 + (g & 3), (g >> 2) * 8 + 4 + (g & 3)):
                rows = packed_s[group, :, part].reshape(64, WIDE)
                packed_s[group, :, part] = mm(order, rows).astype(BF).reshape(4, 16, WIDE)
            for copy in packed_out(g, half):
                copy.start()

    fetch(0).start()
    fetch(1).start()
    edges_in(0).start()
    fetch(2).start()
    for i in range(1, STEPS):
        edges_in(i).start()
    for k in range(3, 6):
        fetch(k).start()
    for i in range(STEPS):
        ecot_in(i).start()

    agg_s[...] = jnp.zeros_like(agg_s)
    dw1_s[...] = jnp.zeros_like(dw1_s)
    dw2_s[...] = jnp.zeros_like(dw2_s)
    gain_s[...] = jnp.zeros_like(gain_s)
    odd_lat, odd_lon = place_ref[1] != 0, place_ref[2] != 0
    lon_a, lon_b, lat_a, lat_b = (
        ref[...].astype(F32) for ref in (lon_a_ref, lon_b_ref, lat_a_ref, lat_b_ref)
    )
    table_s[NODES : NODES + 96] = jnp.concatenate(
        [
            jnp.where(odd_lon, lon_a, lon_b),
            jnp.where(odd_lon, lon_b, lon_a),
            jnp.where(odd_lat, lat_a, lat_b),
            jnp.where(odd_lat, lat_b, lat_a),
        ],
        axis=0,
    ).astype(BF)
    pick = jnp.transpose(jnp.broadcast_to(need_ref[...].astype(F32), (128, 128)))[:, 0:1]
    low, high = far_ref[:, 0].astype(F32), far_ref[:, 1].astype(F32)
    table_s[480:608] = jnp.where(pick == 0.0, low, high).astype(BF)
    table_s[608:SENDERS] = jnp.zeros((32, WIDE), BF)
    fetch(0).wait()
    table_s[0:NODES] = nodes_ref[...]
    fetch(1).wait()
    right_s[0:WIDE] = (ew1_ref[0:WIDE].astype(F32) * 0.5).astype(BF)
    right_s[WIDE : WIDE + ONES_ROW] = (
        mm(table_s[0:ONES_ROW], ew1_ref[WIDE : 2 * WIDE]) * 0.5
    ).astype(BF)
    bias = eb1_ref[...].reshape(1, WIDE) * 0.5
    coarse = bias.astype(BF).astype(F32)
    right_s[WIDE + ONES_ROW : FIRST] = jnp.concatenate(
        [coarse, bias - coarse, jnp.zeros((30, WIDE), F32)], axis=0
    ).astype(BF)
    right_s[FIRST:] = (mm(nodes_ref[...], ew1_ref[2 * WIDE :]) * 0.5).astype(BF)
    fetch(2).wait()
    half_s[...] = (ew2_ref[...].astype(F32) * 0.5).astype(BF)

    def forward(i, carry):
        here = rows_of(i)
        at = i * BLOCK
        slot = lax.broadcasted_iota(jnp.int32, (1, BLOCK), 1) + at
        snd = snd_ref[i].astype(F32)
        rcv = jnp.where(slot < count, rcv_ref[i].astype(F32), -1.0)
        hots = hot_lanes(lane_ids(snd), 0, SENDERS // 128)
        lane = lax.broadcasted_iota(jnp.int32, (BLOCK, 128), 1)
        hots[4] = jnp.where((lane == ONES_ROW - 512) | (lane == ONES_ROW - 511), 1.0, hots[4].astype(F32)).astype(BF)
        hots += hot_lanes(lane_ids(rcv), 0, NODES // 128)
        for k, hot in enumerate(hots):
            left_s[here, WIDE + 128 * k : WIDE + 128 * (k + 1)] = hot
        edges_in(i).wait()
        half = mm(left_s[here], right_s[...])
        t = jnp.tanh(half)
        up = 1.0 + t
        act = (half * up).astype(BF)
        act_s[here] = act
        dact_s[here] = (up * (1.0 + half * (1.0 - t))).astype(BF)
        live = lax.broadcasted_iota(jnp.int32, (BLOCK, 1), 0) + at < count
        z2 = mm(act, ew2_ref[...])
        centred = z2 - row_mean(z2)
        rstd = jnp.where(live, lax.rsqrt(row_mean(centred * centred) + EPS), 0.0)
        normed = centred * rstd
        normed_s[here] = normed.astype(BF)
        rstd_s[here] = jnp.broadcast_to(rstd, (BLOCK, 128))
        fresh = (left_s[here, 0:WIDE].astype(F32) + normed * egain).astype(BF)
        fresh_s[here] = fresh
        fresh_out(i).start()
        agg_s[...] += t_mm(left_s[here, FIRST:], fresh)
        return carry

    lax.fori_loop(0, STEPS, forward, 0)

    for k in range(3, 6):
        fetch(k).wait()
    nodes = nodes_ref[...]
    ngain = ng_ref[...].reshape(1, WIDE)
    agg = agg_s[...].astype(BF)
    z1 = mm(nodes, nw1_ref[0:WIDE]) + mm(agg, nw1_ref[WIDE:]) + nb1_ref[...].reshape(1, WIDE)
    act, dact = first_act(z1)
    act = act.astype(BF)
    normed, rstd = normalise(mm(act, nw2_ref[...]))
    new_nodes_s[...] = (nodes.astype(F32) + normed * ngain).astype(BF)
    give(0).start()
    cot = ncot_ref[...].astype(F32)
    gz2 = norm_back(cot, normed, rstd, ngain).astype(BF)
    gain_grad = jnp.sum(cot * normed, axis=0, keepdims=True)
    gz1 = (mm_t(gz2, nw2_ref[...]) * dact).astype(BF)
    bias_grad = jnp.sum(gz1.astype(F32), axis=0, keepdims=True)
    gagg_s[...] = mm_t(gz1, nw1_ref[WIDE:]).astype(BF)
    give(1).start()
    node_s[...] = cot + mm_t(gz1, nw1_ref[0:WIDE])
    packed_s[0:16, 0:2, 0:16] = t_mm(nodes, gz1).astype(BF).reshape(16, 2, 16, WIDE)
    packed_s[16:32, 0:2, 0:16] = t_mm(agg, gz1).astype(BF).reshape(16, 2, 16, WIDE)
    packed_s[:, 2, 0:16] = t_mm(act, gz2).astype(BF).reshape(GROUPS, 16, WIDE)

    def backward(i, carry):
        here = rows_of(i)
        ecot_in(i).wait()
        g = ecot_s[here].astype(F32) + mm(left_s[here, FIRST:], gagg_s[...])
        normed = normed_s[here].astype(F32)
        gain_s[...] += jnp.sum((g * normed).reshape(BLOCK // 8, 8, WIDE), axis=0)
        gz2 = norm_back(g, normed, rstd_s[here][:, 0:1], egain).astype(BF)
        dw2_s[...] += t_mm(act_s[here], gz2)
        gz1 = (mm_t(gz2, half_s[...]) * dact_s[here].astype(F32)).astype(BF)
        ecot_s[here] = gz1
        gz_out(i).start()
        dw1_s[...] += t_mm(left_s[here], gz1)
        return carry

    lax.fori_loop(0, STEPS, backward, 0)

    packed_s[:, 3, 0:16] = dw2_s[...].astype(BF).reshape(GROUPS, 16, WIDE)
    pack(
        0,
        lambda z, slot: jnp.where(
            slot < 8, 8 * z + slot, jnp.where(slot < 12, 24 + 4 * z + slot, 36 + 4 * z + slot)
        ),
    )
    sent, got = dw1_s[WIDE:FIRST].astype(BF), dw1_s[FIRST:].astype(BF)
    back = mm_t(sent, ew1_ref[WIDE : 2 * WIDE])
    node_s[...] += back[0:NODES] + mm_t(got, ew1_ref[2 * WIDE :])
    give(2).start()
    first = jnp.concatenate(
        [
            dw1_s[0:WIDE].astype(BF),
            t_mm(table_s[...], sent).astype(BF),
            t_mm(nodes, got).astype(BF),
        ],
        axis=0,
    )
    packed_s[:, 0:3, 16:32] = first.reshape(GROUPS, 3, 16, WIDE)
    to = [back[NODES + HALO * k : NODES + HALO * (k + 1)] for k in range(4)]
    back_lon_a_ref[...] = jnp.where(odd_lon, to[0], to[1]).astype(BF)
    back_lon_b_ref[...] = jnp.where(odd_lon, to[1], to[0]).astype(BF)
    back_lat_a_ref[...] = jnp.where(odd_lat, to[2], to[3]).astype(BF)
    back_lat_b_ref[...] = jnp.where(odd_lat, to[3], to[2]).astype(BF)
    vectors = (
        dw1_s[WIDE + ONES_ROW : WIDE + ONES_ROW + 1],
        jnp.sum(gain_s[...], axis=0, keepdims=True),
        bias_grad,
        gain_grad,
    )
    half = WIDE // 2
    paired = [
        jnp.concatenate([vectors[k][:, side], vectors[k + 1][:, side]], axis=1)
        for side in (slice(0, half), slice(half, WIDE))
        for k in (0, 2)
    ]
    extra = jnp.concatenate([back[480:608]] + paired + [jnp.zeros((124, WIDE), F32)], axis=0)
    out = lax.broadcasted_iota(jnp.int32, (GROUPS * 16, 256), 0)
    src = lax.broadcasted_iota(jnp.int32, (GROUPS * 16, 256), 1)
    need = jnp.concatenate([need_ref[...], jnp.zeros((1, 128), jnp.int32)], axis=1)
    slot = out & 15
    low = (slot < 4) & (src == (out >> 4) * 4 + slot) & (need == 0)
    high = (slot >= 4) & (slot < 8) & (src == (out >> 4) * 4 + slot - 4) & (need == 1)
    small = (slot >= 8) & (slot < 10) & (src == 120 + slot + (out >> 8) * 2)
    move = jnp.where(low | high | small, 1.0, 0.0).astype(BF)
    packed_s[:, 3, 16:32] = mm(move, extra.astype(BF)).astype(BF).reshape(GROUPS, 16, WIDE)
    pack(
        1,
        lambda z, slot: jnp.where(
            slot < 12, 12 * z + slot, jnp.where(slot < 14, z + 4 * slot, 42 + slot)
        ),
    )
    for k in range(3):
        give(k).wait()
    for i in range(STEPS):
        fresh_out(i).wait()
        gz_out(i).wait()
    for g in range(16):
        for copy in packed_out(g, 0) + packed_out(g, 1):
            copy.wait()


def layer(place, snd, rcv, need, edges, ecot, nodes, borders, far, ncot, ew1, ew2, nw1, nw2, eb1, eg, nb1, ng):
    sds = jax.ShapeDtypeStruct
    vmem = pl.BlockSpec(memory_space=pltpu.VMEM)
    hbm = pl.BlockSpec(memory_space=pl.ANY)
    return pl.pallas_call(
        layer_kernel,
        name="mesh_layer",
        in_specs=[pl.BlockSpec(memory_space=pltpu.SMEM)] + [vmem] * 12 + [hbm] * 8,
        out_specs=[vmem] * 4 + [hbm] * 7,
        out_shape=[sds((HALO, WIDE), BF)] * 4
        + [
            sds((NODES, WIDE), BF),
            sds((EDGES, WIDE), BF),
            sds((EDGES, WIDE), BF),
            sds((NODES, WIDE), BF),
            sds((NODES, WIDE), F32),
        ]
        + [sds((16, 4, GROUP_ROWS // 4, WIDE), BF)] * 2,
        scratch_shapes=[
            pltpu.VMEM((NODES, WIDE), BF),
            pltpu.VMEM((NODES, WIDE), BF),
            pltpu.VMEM((3 * WIDE, WIDE), BF),
            pltpu.VMEM((WIDE, WIDE), BF),
            pltpu.VMEM((2 * WIDE, WIDE), BF),
            pltpu.VMEM((WIDE, WIDE), BF),
            pltpu.VMEM((SENDERS, WIDE), BF),
            pltpu.VMEM((WIDE + TABLE, WIDE), BF),
            pltpu.VMEM((EDGES, WIDE + TABLE), BF),
            pltpu.VMEM((EDGES, WIDE), BF),
            pltpu.VMEM((EDGES, WIDE), BF),
            pltpu.VMEM((EDGES, WIDE), BF),
            pltpu.VMEM((EDGES, WIDE), BF),
            pltpu.VMEM((EDGES, WIDE), BF),
            pltpu.VMEM((EDGES, 128), F32),
            pltpu.VMEM((NODES, WIDE), BF),
            pltpu.VMEM((NODES, WIDE), BF),
            pltpu.VMEM((NODES, WIDE), F32),
            pltpu.VMEM((NODES, WIDE), F32),
            pltpu.VMEM((WIDE + TABLE, WIDE), F32),
            pltpu.VMEM((WIDE, WIDE), F32),
            pltpu.VMEM((8, WIDE), F32),
            pltpu.VMEM((GROUPS, 4, GROUP_ROWS // 4, WIDE), BF),
            pltpu.VMEM((WIDE, WIDE), BF),
            pltpu.SemaphoreType.DMA((9,)),
            pltpu.SemaphoreType.DMA((STEPS,)),
            pltpu.SemaphoreType.DMA((STEPS,)),
            pltpu.SemaphoreType.DMA((STEPS,)),
            pltpu.SemaphoreType.DMA((STEPS,)),
            pltpu.SemaphoreType.DMA((64,)),
        ],
        compiler_params=pltpu.CompilerParams(vmem_limit_bytes=60 * 1024 * 1024),
        cost_estimate=pl.CostEstimate(
            flops=18 << 30, transcendentals=4 << 20, bytes_accessed=30 << 20
        ),
    )(place, snd, rcv, need, *borders, far, eb1, eg, nb1, ng, edges, ecot, nodes, ncot, ew1, ew2, nw1, nw2)


def edge_grad_kernel(count_ref, rcv_ref, ecot_ref, gz_ref, gagg_ref, ew1_ref, out_ref):
    at = pl.program_id(0) * BLOCK
    back = jnp.concatenate(hot_lanes(lane_ids(rcv_ref[0].astype(F32)), 0, NODES // 128), axis=1)
    live = (lax.broadcasted_iota(jnp.int32, (BLOCK, 1), 0) + at < count_ref[0]).astype(F32)
    taken = live * mm(back, gagg_ref[...])
    out_ref[...] = ecot_ref[...].astype(F32) + taken + mm_t(gz_ref[...], ew1_ref[...])


def edge_grads(place, rcv, ecot, gz, gagg, ew1):
    same = lambda i: i
    return pl.pallas_call(
        edge_grad_kernel,
        name="edge_grads",
        grid=(STEPS,),
        in_specs=[
            pl.BlockSpec(memory_space=pltpu.SMEM),
            by_block((1, 1, BLOCK), same),
            by_block((BLOCK, WIDE), same),
            by_block((BLOCK, WIDE), same),
            whole(NODES, WIDE),
            whole(WIDE, WIDE),
        ],
        out_specs=by_block((BLOCK, WIDE), same),
        out_shape=jax.ShapeDtypeStruct((EDGES, WIDE), F32),
        compiler_params=params(),
        cost_estimate=pl.CostEstimate(
            flops=2 * EDGES * WIDE * (WIDE + NODES), transcendentals=0, bytes_accessed=13 << 20
        ),
    )(place, rcv, ecot, gz, gagg, ew1)


def finish_kernel(lane_ref, total_ref, node_ref, out_ref, *grads):
    total = total_ref[...]
    ew1, eb1, ew2, eg, nw1, nb1, nw2, ng = grads
    nw1[...] = total[0:8]
    nw2[...] = total[8:12]
    ew2[...] = total[12:16]
    ew1[...] = total[16:28]
    out_ref[...] = node_ref[...]
    out_ref[0:COARSE] += total[28:30]
    half = WIDE // 2
    lines = [total[30:31, :half], total[30:31, half:], total[31:32, :half], total[31:32, half:]]
    lines = jnp.concatenate(lines + [jnp.zeros((4, half), F32)], axis=0)
    lines = pltpu.roll(lines, (half - lane_ref[0]) & (half - 1), 1)
    for k, ref in enumerate((eb1, eg, nb1, ng)):
        ref[...] = lines[k, 0:4]


def finish(lane, total, node_grad):
    sds = jax.ShapeDtypeStruct
    rows = [(12, WIDE), (4,), (4, WIDE), (4,), (8, WIDE), (4,), (4, WIDE), (4,)]
    first = pl.BlockSpec((8, WIDE), lambda i: (0, 0))
    return pl.pallas_call(
        finish_kernel,
        name="finish_grads",
        grid=(1,),
        in_specs=[
            pl.BlockSpec(memory_space=pltpu.SMEM),
            whole(GROUP_ROWS // 4, WIDE),
            first,
        ],
        out_specs=[first] + [pl.BlockSpec(r, lambda i, n=len(r): (0,) * n) for r in rows],
        out_shape=[sds((NODES, WIDE), F32)] + [sds(r, F32) for r in rows],
        input_output_aliases={2: 0},
        compiler_params=params(),
    )(lane, total, node_grad)


def swap(block, axis, first, around):
    n = lax.axis_size(axis)
    pairs = [(i, (i + 1) % n) for i in range(first, n, 2) if around or i + 1 < n]
    return lax.ppermute(block, axis, pairs + [(j, i) for i, j in pairs])


def shards(
    nodes,
    edges,
    senders,
    receivers,
    edge_count,
    halo_send,
    long_need,
    node_cot,
    edge_cot,
    e_w1,
    e_b1,
    e_w2,
    e_gain,
    n_w1,
    n_b1,
    n_w2,
    n_gain,
):
    nodes_l, edges_l, ecot = nodes[0, 0], edges[0, 0], edge_cot[0, 0]
    rows_out = halo_send[0, 0]
    snd = senders.reshape(STEPS, 1, BLOCK)
    rcv = receivers.reshape(STEPS, 1, BLOCK)
    far = lax.all_to_all(
        jnp.broadcast_to(nodes_l[None, :COARSE], (FAR, COARSE, WIDE)), LAT_LON, split_axis=0, concat_axis=0, tiled=True)
    place = jnp.stack(
        [
            edge_count[0, 0],
            lax.axis_index("lat_1").astype(jnp.int32),
            (lax.axis_index("lon_1") & 1).astype(jnp.int32),
        ]
    )
    sent = borders(place, nodes_l, rows_out)
    halo = [
        swap(sent[0], LON, 0, True),
        swap(sent[1], LON, 1, True),
        swap(sent[2], LAT, 0, False),
        swap(sent[3], LAT, 1, False),
    ]
    *halo_grad, new_nodes, new_edges, gz, gagg, node_part, keep, send = layer(
        place,
        snd,
        rcv,
        long_need.reshape(1, FAR),
        edges_l,
        ecot,
        nodes_l,
        halo,
        far,
        node_cot[0, 0],
        e_w1,
        e_w2,
        n_w1,
        n_w2,
        e_b1,
        e_gain,
        n_b1,
        n_gain,
    )
    pair = lax.ppermute(send, "lat_1", [(0, 1), (1, 0)])
    both = (keep.astype(F32) + pair.astype(F32)).astype(BF).reshape(64, GROUP_ROWS // 4, WIDE)
    both, halo_grad, gz = lax.optimization_barrier((both, halo_grad, gz))
    parts = lax.all_to_all(
        both, ("lat_0", "lon_0", "lon_1"), split_axis=0, concat_axis=0, tiled=True
    )
    edge_grad = edge_grads(place, rcv, ecot, gz, gagg, e_w1)
    returned = [
        swap(halo_grad[0], LON, 0, True),
        swap(halo_grad[1], LON, 1, True),
        swap(halo_grad[2], LAT, 0, False),
        swap(halo_grad[3], LAT, 1, False),
    ]
    odd = (place[2], 1 - place[2], 2 + place[1], 3 - place[1])
    sorted_rows = jnp.concatenate(
        [lax.dynamic_slice_in_dim(rows_out, k, 1, 0) for k in odd], axis=1
    )
    border = (sorted_rows == lax.broadcasted_iota(jnp.int32, (NODES, 4 * HALO), 0)).astype(BF)
    node_grad = node_part + jnp.dot(border, jnp.concatenate(returned, axis=0), preferred_element_type=F32)
    parts, edge_grad, node_grad = lax.optimization_barrier((parts, edge_grad, node_grad))
    lane = ((lax.axis_index(LAT_LON) & 63) * 4).astype(jnp.int32).reshape(1)
    node_grad, *sums = finish(lane, jnp.sum(parts.astype(F32), axis=0), node_grad)
    return (
        new_nodes[None, None],
        new_edges[None, None],
        node_grad[None, None],
        edge_grad[None, None],
        *sums,
    )


def solution(mesh):
    finer = Mesh(mesh.devices.reshape(4, 2, 4, 4), ("lat_0", "lat_1", "lon_0", "lon_1"))
    placed = (
        P(LAT, LON, None, None),
        P(LAT, LON, None, None),
        P(LAT, LON, None),
        P(LAT, LON, None),
        P(LAT, LON),
        P(LAT, LON, None, None),
        P(LAT, LON, None, None),
        P(LAT, LON, None, None),
        P(LAT, LON, None, None),
        P(),
        P(),
        P(),
        P(),
        P(),
        P(),
        P(),
        P(),
    )
    return jax.shard_map(
        shards,
        mesh=finer,
        in_specs=placed,
        out_specs=(
            P(LAT, LON, None, None),
            P(LAT, LON, None, None),
            P(LAT, LON, None, None),
            P(LAT, LON, None, None),
            P(LAT_LON, None),
            P(LAT_LON),
            P(LAT_LON, None),
            P(LAT_LON),
            P(LAT_LON, None),
            P(LAT_LON),
            P(LAT_LON, None),
            P(LAT_LON),
        ),
        check_vma=False,
    )
```
